256 devices in a mesh: pipe: 4 (over y), req: 16 (over z, core), tp: 4 (over x).
Axes of the slice: x: 4, y: 4, z: 8, core: 2. Of those that a mesh axis runs over, the one named last changes fastest.
Arguments:
- hidden: bfloat16 [2048, 8192], P('req', 'tp'), may hold values from -64 to 64
- queries: bfloat16 [4, 2048, 4096], P('pipe', 'req', 'tp'), may hold values from -32 to 32
- norm_gain: bfloat16 [4, 8192], P('pipe'), may hold values from 0.5 to 1.5
- kv_weight: bfloat16 [4, 8192, 2, 512], P('pipe', None, None, 'tp'), may hold values from -0.0625 to 0.0625
- adapter_in: bfloat16 [4, 64, 64, 4096], P('pipe', 'req', None, 'tp'), may hold values from -0.09375 to 0.09375
- adapter_out: bfloat16 [4, 64, 64, 8192], P('pipe', 'req', None, 'tp'), may hold values from -3 to 3
- kv_pages: bfloat16 [4, 2048, 2, 64, 512], P('pipe', 'req', None, None, 'tp'), may hold values from -4 to 4
- adapter_ids: int32 [512], P('req'), may hold values from 0 to 63, as said below
- owner_rows: int32 [64], replicated, may hold values from 0 to 63, as said below
- page_table: int32 [512, 4], P('req'), may hold values from 0 to 127, as said below
- lengths: int32 [512], P('req'), may hold values from 1 to 252, as said below
- moves: int32 [256, 3], P('req'), may hold values from 0 to 127, as said below
Outputs:
- section_out: bfloat16 [4, 2048, 8192], P('pipe', 'req', 'tp')
- new_kv: bfloat16 [4, 2048, 2, 512], P('pipe', 'req', None, 'tp')
- arrived: bfloat16 [4, 480, 2, 64, 512], P('pipe', 'req', None, None, 'tp')
The draws below stay inside these ranges and needn't reach their ends.
Inputs may be any that keep to these rules, and one draw needn't show every extreme that they name: `adapter_ids`: adapter a is stored at row owner_rows[a], on request device owner_rows[a] // 4. In each aligned block of 16 requests at most 2 requests have adapters stored on one request device, and in every block some device stores exactly 2 of them. `owner_rows`: each storage row once. `page_table`: the 128 slots of one request device are each named once by its requests. `lengths`: every request device has a request of length 252. `moves`: row i * 16 + k belongs to request device i. Its destination differs from i; its source slots are distinct; at most 2 of its rows name one destination, exactly 2 for some; destination slots are below 30 and distinct among all rows that name one destination.
All inputs are finite; a program needn't handle non-finite values.
Results may differ from the reference program's by a relative error of at most 0.02.
Values may be sent and summed in bfloat16 or wider, within the bound.
A program may use at most 128 MiB of HBM per device.

```python
import math
import jax
import jax.numpy as jnp
from jax import lax

D = 8192
HD = 128
QH = 32
KVH = 4
R = 64
ADP_DEV = 4
RQ = 32
S = 4
PAGE = 64
MAXP = 4
MOVES = 16
LAYERS = 4
REQUESTS = 512
TOKENS = 2048
ADAPTERS = 64
RQ_MB = 16
CTX = 256
USED = 128
POOL_ALL = 2048
MOVES_ALL = 256
FREE = 30
FREE_ALL = 480


def owner_perm(key):
    return jax.random.permutation(jax.random.fold_in(key, 11), ADAPTERS).astype(jnp.int32)


def draw_owner_rows(key, part):
    return owner_perm(key)


def draw_adapter_ids(key, part):
    req_count = REQUESTS // RQ
    block_count = REQUESTS // RQ_MB
    block_cap = min(RQ_MB, max(2, 2 * RQ_MB // req_count))
    slot_total = req_count * block_cap
    inverse = jnp.argsort(owner_perm(key)).astype(jnp.int32)
    seed_key = jax.random.fold_in(key, 12)

    def one_block(block_id):
        block_key = jax.random.fold_in(seed_key, block_id)
        key_full, key_score, key_order, key_local = jax.random.split(block_key, 4)
        full_dest = jax.random.randint(key_full, (), 0, req_count)
        slot_ids = jnp.arange(slot_total, dtype=jnp.int32)
        dest_of = slot_ids // block_cap
        scores = jax.random.randint(key_score, (slot_total,), 0, 1 << 20) * slot_total + slot_ids
        scores = jnp.where(dest_of == full_dest, slot_ids - slot_total, scores)
        picked = dest_of[jnp.argsort(scores)[:RQ_MB]]
        picked = picked[jax.random.permutation(key_order, RQ_MB)]
        local_row = jax.random.randint(key_local, (RQ_MB,), 0, ADP_DEV)
        return inverse[picked * ADP_DEV + local_row]
    return jax.vmap(one_block)(jnp.arange(block_count, dtype=jnp.int32)).reshape(REQUESTS).astype(jnp.int32)


def draw_page_table(key, part):
    req_count = REQUESTS // RQ
    key_list = jax.random.split(jax.random.fold_in(key, 31), req_count)
    tables = jax.vmap(lambda one_key: jax.random.permutation(one_key, USED))(key_list)
    return tables.reshape(REQUESTS, MAXP).astype(jnp.int32)


def draw_lengths(key, part):
    req_count = REQUESTS // RQ
    drawn = jax.random.randint(jax.random.fold_in(key, 21), (req_count, RQ), 1, CTX - S + 1)
    longest = jax.random.randint(jax.random.fold_in(key, 22), (req_count, 1), 0, RQ)
    filled = jnp.where(jnp.arange(RQ, dtype=jnp.int32)[None, :] == longest, CTX - S, drawn)
    return filled.reshape(REQUESTS).astype(jnp.int32)


def draw_moves(key, part):
    req_count = REQUESTS // RQ
    span_len = req_count - 1
    cap_pair = (MOVES + req_count - 2) // span_len
    shifts = jax.random.randint(jax.random.fold_in(key, 41), (req_count, 1), 0, span_len)
    source = jnp.arange(req_count, dtype=jnp.int32)[:, None]
    moving = jnp.arange(MOVES, dtype=jnp.int32)[None, :]
    offsets = (moving + shifts) % span_len
    target = (source + 1 + offsets) % req_count
    serial = moving // span_len
    distance = (source - target) % req_count
    landing = (distance - 1) * cap_pair + serial
    key_list = jax.random.split(jax.random.fold_in(key, 42), req_count)
    src_slots = jax.vmap(lambda one_key: jax.random.permutation(one_key, USED)[:MOVES])(key_list)
    return jnp.stack([target, src_slots, landing], axis=-1).reshape(MOVES_ALL, 3).astype(jnp.int32)


def draw_kv_pages(key, part):
    full_shape = (LAYERS, POOL_ALL, 2, PAGE, KVH * HD)
    values = jnp.clip(jax.random.normal(jax.random.fold_in(key, 62), full_shape, jnp.float32), -4.0, 4.0)
    part_scale = jnp.array([0.5, 1.0], jnp.float32).reshape(1, 1, 2, 1, 1)
    values = values * part_scale
    return values.astype(jnp.bfloat16)


def draw_queries(key, part):
    full_shape = (LAYERS, TOKENS, QH * HD)
    values = jnp.clip(2.0 * jax.random.normal(jax.random.fold_in(key, 72), full_shape, jnp.float32), -8.0, 8.0)
    return values.astype(jnp.bfloat16)


def draw_hidden(key, part):
    row_scale = jnp.exp(jax.random.uniform(jax.random.fold_in(key, 82), (TOKENS, 1), jnp.float32, math.log(0.4), math.log(4.0)))
    col_scale = jnp.exp(jax.random.uniform(jax.random.fold_in(key, 83), (1, D), jnp.float32, math.log(0.4), math.log(4.0)))
    base_vals = jnp.clip(jax.random.normal(jax.random.fold_in(key, 85), (TOKENS, D), jnp.float32), -4.0, 4.0)
    return (base_vals * row_scale * col_scale).astype(jnp.bfloat16)


def levels(key, shape, shards, least, largest):
    level = 1.0
    for position, blocks in shards:
        steps = jax.random.uniform(jax.random.fold_in(jax.random.fold_in(key, 6), position), (blocks,), jnp.float32, least / len(shards), largest / len(shards))
        level = level * jnp.repeat(jnp.exp(steps), shape[position] // blocks).reshape((-1,) + (1,) * (len(shape) - 1 - position))
    return level


def scatter_about(key, shape, deviation, reach, cuts=(), kind=jnp.bfloat16):
    values = deviation * jax.random.normal(key, shape, jnp.float32)
    if cuts:
        values = values * levels(key, shape, cuts, -0.22, 0.18)
    return jnp.clip(values, -reach, reach).astype(kind)


def setup_inputs(seed: int = 0) -> dict:
    splits = jax.random.split(jax.random.key(seed), 13)
    return {
        "hidden": draw_hidden(jax.random.fold_in(splits[12], 71), 0),
        "queries": draw_queries(jax.random.fold_in(splits[12], 71), 0),
        "norm_gain": jnp.clip(1.0 + 0.1 * jax.random.normal(splits[2], (LAYERS, D), jnp.float32), 0.5, 1.5).astype(jnp.bfloat16),
        "kv_weight": scatter_about(splits[3], (LAYERS, D, 2, KVH * HD), D ** -0.5, 0.0625, ((0, 4), (3, 4))),
        "adapter_in": scatter_about(splits[4], (LAYERS, ADAPTERS, R, QH * HD), (QH * HD) ** -0.5, 0.09375, ((0, 4), (1, 16), (3, 4))),
        "adapter_out": scatter_about(splits[5], (LAYERS, ADAPTERS, R, D), (R // 16) ** -0.5, 3.0, ((0, 4), (1, 16), (3, 4))),
        "kv_pages": draw_kv_pages(jax.random.fold_in(splits[12], 71), 0),
        "adapter_ids": draw_adapter_ids(jax.random.fold_in(splits[12], 71), 0),
        "owner_rows": draw_owner_rows(jax.random.fold_in(splits[12], 71), 0),
        "page_table": draw_page_table(jax.random.fold_in(splits[12], 71), 0),
        "lengths": draw_lengths(jax.random.fold_in(splits[12], 71), 0),
        "moves": draw_moves(jax.random.fold_in(splits[12], 71), 0),
    }


def rotate(key_vecs, positions):
    half_dim = key_vecs.shape[-1] // 2
    inv_freq = jnp.exp(-math.log(500000.0) * (2.0 * jnp.arange(half_dim, dtype=jnp.float32) / key_vecs.shape[-1]))
    angles = positions.astype(jnp.float32)[..., None, None] * inv_freq
    cos_vals = jnp.cos(angles)
    sin_vals = jnp.sin(angles)
    front_half = key_vecs[..., :half_dim]
    back_half = key_vecs[..., half_dim:]
    return jnp.concatenate([front_half * cos_vals - back_half * sin_vals, back_half * cos_vals + front_half * sin_vals], axis=-1)

def reference(hidden, queries, norm_gain, kv_weight, adapter_in, adapter_out, kv_pages, adapter_ids, owner_rows, page_table, lengths, moves):
    group_size = QH // KVH
    token_ids = jnp.arange(S, dtype=jnp.int32)
    device_base = jnp.arange(REQUESTS, dtype=jnp.int32) // RQ * USED
    global_table = page_table + device_base[:, None]
    positions = (lengths[:, None] + token_ids[None, :]).reshape(TOKENS)
    page_slot = jnp.take_along_axis(global_table, (positions // PAGE).reshape(REQUESTS, S), axis=1).reshape(TOKENS)
    page_offset = positions % PAGE
    store_rows = owner_rows[adapter_ids]
    source_dev = jnp.arange(MOVES_ALL, dtype=jnp.int32) // MOVES
    key_index = jnp.arange(CTX + S, dtype=jnp.int32)
    hstate = hidden
    section_list = []
    fresh_list = []
    arrived_list = []
    for layer_id in range(LAYERS):
        widened = hstate.astype(jnp.float32)
        inv_rms = lax.rsqrt(lax.optimization_barrier(jnp.mean(widened * widened, axis=-1, keepdims=True)) + 1e-05)
        normed = (widened * inv_rms * norm_gain[layer_id].astype(jnp.float32)).astype(jnp.bfloat16)
        projected = jnp.dot(normed, kv_weight[layer_id].reshape(D, 2 * KVH * HD), preferred_element_type=jnp.float32).reshape(TOKENS, 2, KVH, HD)
        new_keys = rotate(projected[:, 0], positions).astype(jnp.bfloat16)
        new_values = projected[:, 1].astype(jnp.bfloat16)
        fresh_kv = jnp.stack([new_keys, new_values], axis=1).reshape(TOKENS, 2, KVH * HD)
        layer_pages = kv_pages[layer_id]

        def attend_one(inputs):
            page_rows, length, query_req, fresh_req = inputs
            gathered = layer_pages[page_rows]
            cached = jnp.swapaxes(gathered, 0, 1).reshape(2, CTX, KVH, HD)
            fresh_heads = fresh_req.reshape(S, 2, KVH, HD)
            key_all = jnp.concatenate([cached[0], fresh_heads[:, 0]], axis=0).astype(jnp.float32)
            value_all = jnp.concatenate([cached[1], fresh_heads[:, 1]], axis=0).astype(jnp.float32)
            query_heads = query_req.reshape(S, KVH, group_size, HD).astype(jnp.float32)
            scores = jnp.einsum('skgd,tkd->skgt', query_heads, key_all) * HD ** (-0.5)
            allowed = jnp.where(key_index[None, :] < CTX, key_index[None, :] < length, key_index[None, :] - CTX <= token_ids[:, None])
            scores = jnp.where(allowed[:, None, None, :], scores, -jnp.inf)
            row_max = lax.optimization_barrier(jnp.max(scores, axis=-1, keepdims=True))
            exp_scores = jnp.exp(scores - row_max)
            weights = (exp_scores / lax.optimization_barrier(jnp.sum(exp_scores, axis=-1, keepdims=True))).astype(jnp.bfloat16)
            mixed = jnp.einsum('skgt,tkd->skgd', weights.astype(jnp.float32), value_all)
            return mixed.reshape(S, QH * HD).astype(jnp.bfloat16)
        attended = lax.map(attend_one, (global_table, lengths, queries[layer_id].reshape(REQUESTS, S, QH * HD), fresh_kv.reshape(REQUESTS, S, 2 * KVH * HD)))

        def adapt_one(inputs):
            store_row, attended_req = inputs
            rank_low = jnp.dot(attended_req, adapter_in[layer_id, store_row].T, preferred_element_type=jnp.float32).astype(jnp.bfloat16)
            return jnp.dot(rank_low, adapter_out[layer_id, store_row], preferred_element_type=jnp.float32).astype(jnp.bfloat16)
        deltas = lax.map(adapt_one, (store_rows, attended)).reshape(TOKENS, D)
        hstate = (hstate.astype(jnp.float32) + deltas.astype(jnp.float32)).astype(jnp.bfloat16)
        section_list.append(hstate)
        fresh_list.append(fresh_kv)
        written = layer_pages.at[page_slot, :, page_offset, :].set(fresh_kv)
        leaving = written[source_dev * USED + moves[:, 1]]
        empty_pages = jnp.zeros((FREE_ALL, 2, PAGE, KVH * HD), jnp.bfloat16)
        arrived_list.append(empty_pages.at[moves[:, 0] * FREE + moves[:, 2]].set(leaving))
    return (jnp.stack(section_list), jnp.stack(fresh_list), jnp.stack(arrived_list))
```

```python
import functools
import math

import jax
import jax.numpy as jnp
from jax import lax
from jax.experimental import pallas as pl
from jax.experimental.pallas import tpu as pltpu
from jax.sharding import PartitionSpec as P

D = 8192
HD = 128
R = 64
ADP_DEV = 4
RQ = 32
S = 4
MICRO = 2
PAGE = 64
MOVES = 16
RQ_MB = 16
CTX = 256


def passed_along(block, axis, distance):
    devices = range(lax.axis_size(axis))
    route = [(i - distance, i) for i in devices if i - distance in devices]
    return lax.ppermute(block, axis, route)


def exchange_kernel(axis, n, gather, x_ref, o_ref, send_sem, recv_sem, local_sem):
    me = lax.axis_index(axis)
    barrier = pltpu.get_barrier_semaphore()
    for j in range(1, n):
        pl.semaphore_signal(
            barrier, 1, device_id={axis: (me + j) % n}, device_id_type=pl.DeviceIdType.MESH
        )
    pl.semaphore_wait(barrier, n - 1)
    copies = []
    for j in range(1, n):
        peer = (me + j) % n
        copy = pltpu.make_async_remote_copy(
            src_ref=x_ref if gather else x_ref.at[peer],
            dst_ref=o_ref.at[me],
            send_sem=send_sem.at[j],
            recv_sem=recv_sem.at[j],
            device_id={axis: peer},
            device_id_type=pl.DeviceIdType.MESH,
        )
        copy.start()
        copies.append(copy)
    local = pltpu.make_async_copy(x_ref if gather else x_ref.at[me], o_ref.at[me], local_sem)
    local.start()
    local.wait()
    for copy in copies:
        copy.wait()


def exchange(x, axis, collective_id, gather=False):
    n = lax.axis_size(axis)
    out_shape = (n,) + x.shape if gather else x.shape
    return pl.pallas_call(
        functools.partial(exchange_kernel, axis, n, gather),
        out_shape=jax.ShapeDtypeStruct(out_shape, x.dtype),
        in_specs=[pl.BlockSpec(memory_space=pl.ANY)],
        out_specs=pl.BlockSpec(memory_space=pl.ANY),
        scratch_shapes=[
            pltpu.SemaphoreType.DMA((n,)),
            pltpu.SemaphoreType.DMA((n,)),
            pltpu.SemaphoreType.DMA(()),
        ],
        compiler_params=pltpu.CompilerParams(collective_id=collective_id, has_side_effects=True),
    )(x)


def rotate(key_vecs, positions):
    half_dim = key_vecs.shape[-1] // 2
    inv_freq = jnp.exp(
        -math.log(500000.0) * (2.0 * jnp.arange(half_dim, dtype=jnp.float32) / key_vecs.shape[-1])
    )
    angles = positions.astype(jnp.float32)[..., None, None] * inv_freq
    cos_vals = jnp.cos(angles)
    sin_vals = jnp.sin(angles)
    front_half = key_vecs[..., :half_dim]
    back_half = key_vecs[..., half_dim:]
    return jnp.concatenate(
        [
            front_half * cos_vals - back_half * sin_vals,
            back_half * cos_vals + front_half * sin_vals,
        ],
        axis=-1,
    )


def body(
    hidden,
    queries,
    norm_gain,
    kv_weight,
    adapter_in,
    adapter_out,
    kv_pages,
    adapter_ids,
    owner_rows,
    page_table,
    lengths,
    moves,
):
    section_count = lax.axis_size("pipe")
    req_count = lax.axis_size("req")
    section_id = lax.axis_index("pipe")
    my_req = lax.axis_index("req")
    width_loc = hidden.shape[1]
    q_width = queries.shape[2]
    kv_width = kv_weight.shape[3]
    kv_heads = kv_width // HD
    group_size = q_width // HD // kv_heads
    batches = 1
    per_batch = RQ // batches
    rows_per = per_batch * S
    block_cap = min(RQ_MB, max(2, 2 * RQ_MB // req_count))
    batch_cap = block_cap * (MICRO // batches)
    pair_cap = (MOVES + req_count - 2) // (req_count - 1)
    free_slots = (req_count - 1) * pair_cap
    token_ids = jnp.arange(S, dtype=jnp.int32)
    store_rows = owner_rows[adapter_ids]
    dest_all = store_rows // ADP_DEV
    pick_all = store_rows % ADP_DEV
    req_ids = jnp.arange(RQ, dtype=jnp.int32)
    earlier = (
        (req_ids[None, :] < req_ids[:, None])
        & (req_ids[None, :] // per_batch == req_ids[:, None] // per_batch)
        & (dest_all[None, :] == dest_all[:, None])
    )
    slot_all = jnp.sum(earlier.astype(jnp.int32), axis=1)
    positions = (lengths[:, None] + token_ids[None, :]).reshape(RQ * S)
    gain_full = norm_gain[0].astype(jnp.float32)
    weight_flat = kv_weight[0].reshape(D, 2 * kv_width)
    layer_pages = kv_pages[0]
    adapters_in = adapter_in[0]
    adapters_out = adapter_out[0].reshape(ADP_DEV * R, width_loc)
    key_pos = jnp.arange(CTX, dtype=jnp.int32)
    causal = token_ids[None, :] <= token_ids[:, None]
    adapter_slots = jnp.arange(ADP_DEV, dtype=jnp.int32)
    picks_out = jnp.zeros((req_count, batch_cap), jnp.int32).at[dest_all, slot_all].set(pick_all)
    picks_in = lax.all_to_all(picks_out, "req", split_axis=0, concat_axis=0, tiled=True)
    carried = jnp.zeros((rows_per, width_loc), jnp.bfloat16)
    section_rows = jnp.zeros((RQ * S, width_loc), jnp.bfloat16)
    fresh_rows = jnp.zeros((RQ * S, 2, kv_width), jnp.bfloat16)
    for tick_id in range(batches + section_count - 1):
        offset_batch = tick_id - section_id
        active = (offset_batch >= 0) & (offset_batch < batches)
        hstate = jnp.where(section_id == 0, hidden, carried)
        whole_rows = lax.all_gather(hstate, "tp", axis=1, tiled=True)
        widened = whole_rows.astype(jnp.float32)
        inv_rms = lax.rsqrt(jnp.mean(widened * widened, axis=-1, keepdims=True) + 1e-05)
        normed = (widened * inv_rms * gain_full).astype(jnp.bfloat16)
        projected = jnp.dot(normed, weight_flat, preferred_element_type=jnp.float32).reshape(
            rows_per, 2, kv_heads, HD
        )
        new_keys = rotate(projected[:, 0], positions).astype(jnp.bfloat16)
        new_values = projected[:, 1].astype(jnp.bfloat16)
        fresh_kv = jnp.stack(
            [new_keys.reshape(rows_per, kv_width), new_values.reshape(rows_per, kv_width)], axis=1
        )
        gathered = layer_pages[page_table]
        cached = jnp.swapaxes(gathered, 1, 2).reshape(per_batch, 2, CTX, kv_heads, HD)
        fresh_heads = fresh_kv.reshape(per_batch, S, 2, kv_heads, HD)
        query_heads = queries[0].reshape(per_batch, S, kv_heads, group_size, HD)
        score_old = jnp.einsum(
            "bskgd,btkd->bskgt", query_heads, cached[:, 0], preferred_element_type=jnp.float32
        ) * HD ** (-0.5)
        score_new = jnp.einsum(
            "bskgd,btkd->bskgt",
            query_heads,
            fresh_heads[:, :, 0],
            preferred_element_type=jnp.float32,
        ) * HD ** (-0.5)
        old_ok = key_pos[None, :] < lengths[:, None]
        score_old = jnp.where(old_ok[:, None, None, None, :], score_old, -jnp.inf)
        score_new = jnp.where(causal[None, :, None, None, :], score_new, -jnp.inf)
        row_max = jnp.maximum(jnp.max(score_old, axis=-1), jnp.max(score_new, axis=-1))[..., None]
        exp_old = jnp.exp(score_old - row_max)
        exp_new = jnp.exp(score_new - row_max)
        denominator = (jnp.sum(exp_old, axis=-1) + jnp.sum(exp_new, axis=-1))[..., None]
        weight_old = (exp_old / denominator).astype(jnp.bfloat16)
        weight_new = (exp_new / denominator).astype(jnp.bfloat16)
        mixed = jnp.einsum(
            "bskgt,btkd->bskgd", weight_old, cached[:, 1], preferred_element_type=jnp.float32
        )
        mixed = mixed + jnp.einsum(
            "bskgt,btkd->bskgd",
            weight_new,
            fresh_heads[:, :, 1],
            preferred_element_type=jnp.float32,
        )
        attended = mixed.reshape(per_batch, S, q_width).astype(jnp.bfloat16)
        outgoing = (
            jnp.zeros((req_count, batch_cap, S, q_width), jnp.bfloat16)
            .at[dest_all, slot_all]
            .set(attended)
        )
        rows_in = exchange(outgoing, "req", 0)
        sources = rows_in.shape[0]
        item_count = rows_in.shape[1]
        flat_rows = rows_in.reshape(sources * item_count * S, q_width)
        all_low = jnp.einsum(
            "nf,arf->nar", flat_rows, adapters_in, preferred_element_type=jnp.float32
        )
        picks_rows = jnp.broadcast_to(picks_in[:, :, None], (sources, item_count, S)).reshape(
            sources * item_count * S
        )
        one_hot = (picks_rows[:, None] == adapter_slots[None, :]).astype(jnp.float32)
        partial_low = jnp.sum(all_low * one_hot[:, :, None], axis=1)
        rank_low = jnp.sum(exchange(partial_low, "tp", 1, gather=True), axis=0).astype(jnp.bfloat16)
        spread = (rank_low.astype(jnp.float32)[:, None, :] * one_hot[:, :, None]).astype(
            jnp.bfloat16
        )
        deltas = jnp.dot(
            spread.reshape(sources * item_count * S, ADP_DEV * R),
            adapters_out,
            preferred_element_type=jnp.float32,
        ).astype(jnp.bfloat16)
        deltas = deltas.reshape(sources, item_count, S, width_loc)
        returned = exchange(deltas, "req", 2)
        delta_rows = returned[dest_all, slot_all].reshape(rows_per, width_loc)
        new_state = (hstate.astype(jnp.float32) + delta_rows.astype(jnp.float32)).astype(
            jnp.bfloat16
        )
        section_rows = jnp.where(active, new_state, section_rows)
        fresh_rows = jnp.where(active, fresh_kv, fresh_rows)
        carried = passed_along(new_state, "pipe", 1)
    page_slot = jnp.take_along_axis(page_table, (positions // PAGE).reshape(RQ, S), axis=1).reshape(
        RQ * S
    )
    written = layer_pages.at[page_slot, :, positions % PAGE, :].set(fresh_rows)
    leaving = written[moves[:, 1]]
    empty_pages = jnp.zeros((free_slots, 2, PAGE, kv_width), jnp.bfloat16)
    received, dest_in, spots_in = (
        lax.all_gather(leaving, "req", axis=0, tiled=True),
        lax.all_gather(moves[:, 0], "req", axis=0, tiled=True),
        lax.all_gather(moves[:, 2], "req", axis=0, tiled=True),
    )
    target = jnp.where(dest_in == my_req, spots_in, free_slots)
    arrived = empty_pages.at[target].set(received, mode="drop")
    return (section_rows[None], fresh_rows[None], arrived[None])


def solution(mesh):
    in_specs = (
        P("req", "tp"),
        P("pipe", "req", "tp"),
        P("pipe", None),
        P("pipe", None, None, "tp"),
        P("pipe", "req", None, "tp"),
        P("pipe", "req", None, "tp"),
        P("pipe", "req", None, None, "tp"),
        P("req"),
        P(),
        P("req", None),
        P("req"),
        P("req", None),
    )
    out_specs = (
        P("pipe", "req", "tp"),
        P("pipe", "req", None, "tp"),
        P("pipe", "req", None, None, "tp"),
    )
    return jax.shard_map(body, mesh=mesh, in_specs=in_specs, out_specs=out_specs, check_vma=False)
```

```python
import functools
import math

import jax
import jax.numpy as jnp
from jax import lax
from jax.experimental import pallas as pl
from jax.experimental.pallas import tpu as pltpu
from jax.sharding import PartitionSpec as P

D = 8192
HD = 128
R = 64
ADP_DEV = 4
RQ = 32
S = 4
MICRO = 2
PAGE = 64
MOVES = 16
RQ_MB = 16
CTX = 256


def passed_along(block, axis, source):
    return lax.ppermute(block, axis, [(source, source + 1)])


def exchange_kernel(axis, n, gather, gate, x_ref, o_ref, send_sem, recv_sem, local_sem):
    if gate is None:
        exchange_body(axis, n, gather, x_ref, o_ref, send_sem, recv_sem, local_sem)
    else:
        pl.when(lax.axis_index("pipe") == gate)(
            lambda: exchange_body(axis, n, gather, x_ref, o_ref, send_sem, recv_sem, local_sem)
        )


def exchange_body(axis, n, gather, x_ref, o_ref, send_sem, recv_sem, local_sem):
    me = lax.axis_index(axis)
    barrier = pltpu.get_barrier_semaphore()
    for j in range(1, n):
        pl.semaphore_signal(
            barrier, 1, device_id={axis: (me + j) % n}, device_id_type=pl.DeviceIdType.MESH
        )
    pl.semaphore_wait(barrier, n - 1)
    copies = []
    for j in range(1, n):
        peer = (me + j) % n
        copy = pltpu.make_async_remote_copy(
            src_ref=x_ref if gather else x_ref.at[peer],
            dst_ref=o_ref.at[me],
            send_sem=send_sem.at[j],
            recv_sem=recv_sem.at[j],
            device_id={axis: peer},
            device_id_type=pl.DeviceIdType.MESH,
        )
        copy.start()
        copies.append(copy)
    local = pltpu.make_async_copy(x_ref if gather else x_ref.at[me], o_ref.at[me], local_sem)
    local.start()
    local.wait()
    for copy in copies:
        copy.wait()


def exchange(x, axis, collective_id, gather=False, gate=None):
    n = lax.axis_size(axis)
    out_shape = (n,) + x.shape if gather else x.shape
    return pl.pallas_call(
        functools.partial(exchange_kernel, axis, n, gather, gate),
        out_shape=jax.ShapeDtypeStruct(out_shape, x.dtype),
        in_specs=[pl.BlockSpec(memory_space=pl.ANY)],
        out_specs=pl.BlockSpec(memory_space=pl.ANY),
        scratch_shapes=[
            pltpu.SemaphoreType.DMA((n,)),
            pltpu.SemaphoreType.DMA((n,)),
            pltpu.SemaphoreType.DMA(()),
        ],
        compiler_params=pltpu.CompilerParams(collective_id=collective_id, has_side_effects=True),
    )(x)


def rotate(key_vecs, positions):
    half_dim = key_vecs.shape[-1] // 2
    inv_freq = jnp.exp(
        -math.log(500000.0) * (2.0 * jnp.arange(half_dim, dtype=jnp.float32) / key_vecs.shape[-1])
    )
    angles = positions.astype(jnp.float32)[..., None, None] * inv_freq
    cos_vals = jnp.cos(angles)
    sin_vals = jnp.sin(angles)
    front_half = key_vecs[..., :half_dim]
    back_half = key_vecs[..., half_dim:]
    return jnp.concatenate(
        [
            front_half * cos_vals - back_half * sin_vals,
            back_half * cos_vals + front_half * sin_vals,
        ],
        axis=-1,
    )


def body(
    hidden,
    queries,
    norm_gain,
    kv_weight,
    adapter_in,
    adapter_out,
    kv_pages,
    adapter_ids,
    owner_rows,
    page_table,
    lengths,
    moves,
):
    section_count = lax.axis_size("pipe")
    req_count = lax.axis_size("req")
    section_id = lax.axis_index("pipe")
    my_req = lax.axis_index("req")
    width_loc = hidden.shape[1]
    q_width = queries.shape[2]
    kv_width = kv_weight.shape[3]
    kv_heads = kv_width // HD
    group_size = q_width // HD // kv_heads
    batches = 1
    per_batch = RQ // batches
    rows_per = per_batch * S
    block_cap = min(RQ_MB, max(2, 2 * RQ_MB // req_count))
    batch_cap = block_cap * (MICRO // batches)
    pair_cap = (MOVES + req_count - 2) // (req_count - 1)
    free_slots = (req_count - 1) * pair_cap
    token_ids = jnp.arange(S, dtype=jnp.int32)
    store_rows = owner_rows[adapter_ids]
    dest_all = store_rows // ADP_DEV
    pick_all = store_rows % ADP_DEV
    req_ids = jnp.arange(RQ, dtype=jnp.int32)
    earlier = (
        (req_ids[None, :] < req_ids[:, None])
        & (req_ids[None, :] // per_batch == req_ids[:, None] // per_batch)
        & (dest_all[None, :] == dest_all[:, None])
    )
    slot_all = jnp.sum(earlier.astype(jnp.int32), axis=1)
    positions = (lengths[:, None] + token_ids[None, :]).reshape(RQ * S)
    gain_full = norm_gain[0].astype(jnp.float32)
    weight_flat = kv_weight[0].reshape(D, 2 * kv_width)
    layer_pages = kv_pages[0]
    adapters_in = adapter_in[0]
    adapters_out = adapter_out[0].reshape(ADP_DEV * R, width_loc)
    key_pos = jnp.arange(CTX, dtype=jnp.int32)
    causal = token_ids[None, :] <= token_ids[:, None]
    adapter_slots = jnp.arange(ADP_DEV, dtype=jnp.int32)
    move_ids = jnp.arange(MOVES, dtype=jnp.int32)
    move_dest = moves[:, 0]
    move_slot = jnp.sum(
        (
            (move_ids[None, :] < move_ids[:, None]) & (move_dest[None, :] == move_dest[:, None])
        ).astype(jnp.int32),
        axis=1,
    )
    picks_out = jnp.zeros((req_count, batch_cap), jnp.int32).at[dest_all, slot_all].set(pick_all)
    spots_out = jnp.full((req_count, pair_cap), -1, jnp.int32).at[move_dest, move_slot].set(moves[:, 2])
    ints_in = lax.all_to_all(
        jnp.concatenate([picks_out, spots_out], axis=1), "req", split_axis=0, concat_axis=0, tiled=True
    )
    picks_in = ints_in[:, :batch_cap]
    spots_in = ints_in[:, batch_cap:].reshape(req_count * pair_cap)
    spot_match = spots_in[None, :] == jnp.arange(free_slots, dtype=jnp.int32)[:, None]
    has_page = jnp.any(spot_match, axis=1)
    page_src = jnp.argmax(spot_match, axis=1)
    out_pages = (
        jnp.zeros((req_count, pair_cap, 2, PAGE, kv_width), jnp.bfloat16)
        .at[move_dest, move_slot]
        .set(layer_pages[moves[:, 1]])
    )
    page_slot = jnp.take_along_axis(page_table, (positions // PAGE).reshape(RQ, S), axis=1).reshape(
        RQ * S
    )
    tok_move = jnp.argmax(page_slot[:, None] == moves[None, :, 1], axis=1)
    tok_moved = jnp.any(page_slot[:, None] == moves[None, :, 1], axis=1)
    tok_dest = jnp.where(tok_moved, move_dest[tok_move], req_count)
    tok_slot = move_slot[tok_move]
    arrived = jnp.zeros((free_slots, 2, PAGE, kv_width), jnp.bfloat16)
    carried = jnp.zeros((rows_per, width_loc), jnp.bfloat16)
    section_rows = jnp.zeros((RQ * S, width_loc), jnp.bfloat16)
    fresh_rows = jnp.zeros((RQ * S, 2, kv_width), jnp.bfloat16)
    for tick_id in range(batches + section_count - 1):
        offset_batch = tick_id - section_id
        active = (offset_batch >= 0) & (offset_batch < batches)
        hstate = jnp.where(section_id == 0, hidden, carried)
        whole_rows = lax.all_gather(hstate, "tp", axis=1, tiled=True)
        widened = whole_rows.astype(jnp.float32)
        inv_rms = lax.rsqrt(jnp.mean(widened * widened, axis=-1, keepdims=True) + 1e-05)
        normed = (widened * inv_rms * gain_full).astype(jnp.bfloat16)
        projected = jnp.dot(normed, weight_flat, preferred_element_type=jnp.float32).reshape(
            rows_per, 2, kv_heads, HD
        )
        new_keys = rotate(projected[:, 0], positions).astype(jnp.bfloat16)
        new_values = projected[:, 1].astype(jnp.bfloat16)
        fresh_kv = jnp.stack(
            [new_keys.reshape(rows_per, kv_width), new_values.reshape(rows_per, kv_width)], axis=1
        )
        gathered = layer_pages[page_table]
        cached = jnp.swapaxes(gathered, 1, 2).reshape(per_batch, 2, CTX, kv_heads, HD)
        fresh_heads = fresh_kv.reshape(per_batch, S, 2, kv_heads, HD)
        query_heads = queries[0].reshape(per_batch, S, kv_heads, group_size, HD)
        score_old = jnp.einsum(
            "bskgd,btkd->bskgt", query_heads, cached[:, 0], preferred_element_type=jnp.float32
        ) * HD ** (-0.5)
        score_new = jnp.einsum(
            "bskgd,btkd->bskgt",
            query_heads,
            fresh_heads[:, :, 0],
            preferred_element_type=jnp.float32,
        ) * HD ** (-0.5)
        old_ok = key_pos[None, :] < lengths[:, None]
        score_old = jnp.where(old_ok[:, None, None, None, :], score_old, -jnp.inf)
        score_new = jnp.where(causal[None, :, None, None, :], score_new, -jnp.inf)
        row_max = jnp.maximum(jnp.max(score_old, axis=-1), jnp.max(score_new, axis=-1))[..., None]
        exp_old = jnp.exp(score_old - row_max)
        exp_new = jnp.exp(score_new - row_max)
        denominator = (jnp.sum(exp_old, axis=-1) + jnp.sum(exp_new, axis=-1))[..., None]
        weight_old = (exp_old / denominator).astype(jnp.bfloat16)
        weight_new = (exp_new / denominator).astype(jnp.bfloat16)
        mixed = jnp.einsum(
            "bskgt,btkd->bskgd", weight_old, cached[:, 1], preferred_element_type=jnp.float32
        )
        mixed = mixed + jnp.einsum(
            "bskgt,btkd->bskgd",
            weight_new,
            fresh_heads[:, :, 1],
            preferred_element_type=jnp.float32,
        )
        attended = mixed.reshape(per_batch, S, q_width).astype(jnp.bfloat16)
        outgoing = (
            jnp.zeros((req_count, batch_cap, S, q_width), jnp.bfloat16)
            .at[dest_all, slot_all]
            .set(attended)
        )
        rows_in = exchange(outgoing, "req", 0)
        sources = rows_in.shape[0]
        item_count = rows_in.shape[1]
        flat_rows = rows_in.reshape(sources * item_count * S, q_width)
        all_low = jnp.einsum(
            "nf,arf->nar", flat_rows, adapters_in, preferred_element_type=jnp.float32
        )
        picks_rows = jnp.broadcast_to(picks_in[:, :, None], (sources, item_count, S)).reshape(
            sources * item_count * S
        )
        one_hot = (picks_rows[:, None] == adapter_slots[None, :]).astype(jnp.float32)
        partial_low = jnp.sum(all_low * one_hot[:, :, None], axis=1)
        rank_low = jnp.sum(exchange(partial_low, "tp", 1, gather=True), axis=0).astype(jnp.bfloat16)
        spread = (rank_low.astype(jnp.float32)[:, None, :] * one_hot[:, :, None]).astype(
            jnp.bfloat16
        )
        deltas = jnp.dot(
            spread.reshape(sources * item_count * S, ADP_DEV * R),
            adapters_out,
            preferred_element_type=jnp.float32,
        ).astype(jnp.bfloat16)
        deltas = deltas.reshape(sources, item_count, S, width_loc)
        returned = exchange(deltas, "req", 2)
        delta_rows = returned[dest_all, slot_all].reshape(rows_per, width_loc)
        new_state = (hstate.astype(jnp.float32) + delta_rows.astype(jnp.float32)).astype(
            jnp.bfloat16
        )
        section_rows = jnp.where(active, new_state, section_rows)
        fresh_rows = jnp.where(active, fresh_kv, fresh_rows)
        if tick_id + 1 < section_count:
            carried = passed_along(new_state, "pipe", tick_id)
        sent_pages = out_pages.at[tok_dest, tok_slot, :, positions % PAGE, :].set(
            fresh_kv, mode="drop"
        )
        got_pages = exchange(sent_pages, "req", 3 + tick_id, gate=tick_id).reshape(
            req_count * pair_cap, 2, PAGE, kv_width
        )
        landed = jnp.where(
            has_page[:, None, None, None], got_pages[page_src], jnp.zeros((), jnp.bfloat16)
        )
        arrived = jnp.where(section_id == tick_id, landed, arrived)
    return (section_rows[None], fresh_rows[None], arrived[None])


def solution(mesh):
    in_specs = (
        P("req", "tp"),
        P("pipe", "req", "tp"),
        P("pipe", None),
        P("pipe", None, None, "tp"),
        P("pipe", "req", None, "tp"),
        P("pipe", "req", None, "tp"),
        P("pipe", "req", None, None, "tp"),
        P("req"),
        P(),
        P("req", None),
        P("req"),
        P("req", None),
    )
    out_specs = (
        P("pipe", "req", "tp"),
        P("pipe", "req", None, "tp"),
        P("pipe", "req", None, None, "tp"),
    )
    return jax.shard_map(body, mesh=mesh, in_specs=in_specs, out_specs=out_specs, check_vma=False)
```

```python
import functools
import math

import jax
import jax.numpy as jnp
from jax import lax
from jax.experimental import pallas as pl
from jax.experimental.pallas import tpu as pltpu
from jax.sharding import PartitionSpec as P

D = 8192
HD = 128
R = 64
ADP_DEV = 4
RQ = 32
S = 4
MICRO = 2
PAGE = 64
MOVES = 16
RQ_MB = 16
CTX = 256


def passed_along(block, axis, source):
    return lax.ppermute(block, axis, [(source, source + 1)])


def exchange_kernel(axis, n, gather, gate, x_ref, o_ref, send_sem, recv_sem, local_sem):
    if gate is None:
        exchange_body(axis, n, gather, x_ref, o_ref, send_sem, recv_sem, local_sem)
    else:
        pl.when(lax.axis_index("pipe") == gate)(
            lambda: exchange_body(axis, n, gather, x_ref, o_ref, send_sem, recv_sem, local_sem)
        )


def exchange_body(axis, n, gather, x_ref, o_ref, send_sem, recv_sem, local_sem):
    me = lax.axis_index(axis)
    barrier = pltpu.get_barrier_semaphore()
    for j in range(1, n):
        pl.semaphore_signal(
            barrier, 1, device_id={axis: (me + j) % n}, device_id_type=pl.DeviceIdType.MESH
        )
    pl.semaphore_wait(barrier, n - 1)
    copies = []
    for j in range(1, n):
        peer = (me + j) % n
        copy = pltpu.make_async_remote_copy(
            src_ref=x_ref if gather else x_ref.at[peer],
            dst_ref=o_ref.at[me],
            send_sem=send_sem.at[j],
            recv_sem=recv_sem.at[j],
            device_id={axis: peer},
            device_id_type=pl.DeviceIdType.MESH,
        )
        copy.start()
        copies.append(copy)
    local = pltpu.make_async_copy(x_ref if gather else x_ref.at[me], o_ref.at[me], local_sem)
    local.start()
    local.wait()
    for copy in copies:
        copy.wait()


def exchange(x, axis, collective_id, gather=False, gate=None):
    n = lax.axis_size(axis)
    out_shape = (n,) + x.shape if gather else x.shape
    return pl.pallas_call(
        functools.partial(exchange_kernel, axis, n, gather, gate),
        out_shape=jax.ShapeDtypeStruct(out_shape, x.dtype),
        in_specs=[pl.BlockSpec(memory_space=pl.ANY)],
        out_specs=pl.BlockSpec(memory_space=pl.ANY),
        scratch_shapes=[
            pltpu.SemaphoreType.DMA((n,)),
            pltpu.SemaphoreType.DMA((n,)),
            pltpu.SemaphoreType.DMA(()),
        ],
        compiler_params=pltpu.CompilerParams(collective_id=collective_id, has_side_effects=True),
    )(x)


def rotate(key_vecs, positions):
    half_dim = key_vecs.shape[-1] // 2
    inv_freq = jnp.exp(
        -math.log(500000.0) * (2.0 * jnp.arange(half_dim, dtype=jnp.float32) / key_vecs.shape[-1])
    )
    angles = positions.astype(jnp.float32)[..., None, None] * inv_freq
    cos_vals = jnp.cos(angles)
    sin_vals = jnp.sin(angles)
    front_half = key_vecs[..., :half_dim]
    back_half = key_vecs[..., half_dim:]
    return jnp.concatenate(
        [
            front_half * cos_vals - back_half * sin_vals,
            back_half * cos_vals + front_half * sin_vals,
        ],
        axis=-1,
    )


def body(
    hidden,
    queries,
    norm_gain,
    kv_weight,
    adapter_in,
    adapter_out,
    kv_pages,
    adapter_ids,
    owner_rows,
    page_table,
    lengths,
    moves,
):
    section_count = lax.axis_size("pipe")
    req_count = lax.axis_size("req")
    section_id = lax.axis_index("pipe")
    my_req = lax.axis_index("req")
    width_loc = hidden.shape[1]
    q_width = queries.shape[2]
    kv_width = kv_weight.shape[3]
    kv_heads = kv_width // HD
    group_size = q_width // HD // kv_heads
    batches = 1
    per_batch = RQ // batches
    rows_per = per_batch * S
    block_cap = min(RQ_MB, max(2, 2 * RQ_MB // req_count))
    batch_cap = block_cap * (MICRO // batches)
    pair_cap = (MOVES + req_count - 2) // (req_count - 1)
    free_slots = (req_count - 1) * pair_cap
    token_ids = jnp.arange(S, dtype=jnp.int32)
    store_rows = owner_rows[adapter_ids]
    dest_all = store_rows // ADP_DEV
    pick_all = store_rows % ADP_DEV
    req_ids = jnp.arange(RQ, dtype=jnp.int32)
    earlier = (
        (req_ids[None, :] < req_ids[:, None])
        & (req_ids[None, :] // per_batch == req_ids[:, None] // per_batch)
        & (dest_all[None, :] == dest_all[:, None])
    )
    slot_all = jnp.sum(earlier.astype(jnp.int32), axis=1)
    positions = (lengths[:, None] + token_ids[None, :]).reshape(RQ * S)
    gain_full = norm_gain[0].astype(jnp.float32)
    weight_flat = kv_weight[0].reshape(D, 2 * kv_width)
    layer_pages = kv_pages[0]
    adapters_in = adapter_in[0]
    adapters_out = adapter_out[0].reshape(ADP_DEV * R, width_loc)
    key_pos = jnp.arange(CTX, dtype=jnp.int32)
    causal = token_ids[None, :] <= token_ids[:, None]
    adapter_slots = jnp.arange(ADP_DEV, dtype=jnp.int32)
    move_ids = jnp.arange(MOVES, dtype=jnp.int32)
    move_dest = moves[:, 0]
    move_slot = jnp.sum(
        (
            (move_ids[None, :] < move_ids[:, None]) & (move_dest[None, :] == move_dest[:, None])
        ).astype(jnp.int32),
        axis=1,
    )
    picks_out = jnp.zeros((req_count, batch_cap), jnp.int32).at[dest_all, slot_all].set(pick_all)
    spots_out = jnp.full((req_count, pair_cap), -1, jnp.int32).at[move_dest, move_slot].set(moves[:, 2])
    ints_in = lax.all_to_all(
        jnp.concatenate([picks_out, spots_out], axis=1), "req", split_axis=0, concat_axis=0, tiled=True
    )
    picks_in = ints_in[:, :batch_cap]
    spots_in = ints_in[:, batch_cap:].reshape(req_count * pair_cap)
    spot_match = spots_in[None, :] == jnp.arange(free_slots, dtype=jnp.int32)[:, None]
    has_page = jnp.any(spot_match, axis=1)
    page_src = jnp.argmax(spot_match, axis=1)
    box_ids = jnp.arange(req_count * pair_cap, dtype=jnp.int32)
    box_match = (move_dest * pair_cap + move_slot)[None, :] == box_ids[:, None]
    box_move = jnp.argmax(box_match, axis=1)
    box_used = jnp.any(box_match, axis=1)
    box_page = jnp.where(box_used, moves[box_move, 1], -1)
    out_pages = jnp.where(
        box_used[:, None, None, None], layer_pages[moves[box_move, 1]], jnp.zeros((), jnp.bfloat16)
    )
    page_slot = jnp.take_along_axis(page_table, (positions // PAGE).reshape(RQ, S), axis=1).reshape(
        RQ * S
    )
    spot_ids = jnp.arange(req_count * pair_cap * PAGE, dtype=jnp.int32)
    tok_match = (
        (page_slot[None, :] == box_page[spot_ids // PAGE][:, None])
        & ((positions % PAGE)[None, :] == (spot_ids % PAGE)[:, None])
    )
    tok_pick = tok_match.astype(jnp.bfloat16)
    tok_hit = jnp.any(tok_match, axis=1).reshape(req_count * pair_cap, PAGE)
    carried = jnp.zeros((rows_per, width_loc), jnp.bfloat16)
    section_rows = jnp.zeros((RQ * S, width_loc), jnp.bfloat16)
    fresh_rows = jnp.zeros((RQ * S, 2, kv_width), jnp.bfloat16)
    for tick_id in range(batches + section_count - 1):
        offset_batch = tick_id - section_id
        active = (offset_batch >= 0) & (offset_batch < batches)
        hstate = jnp.where(section_id == 0, hidden, carried)
        whole_rows = lax.all_gather(hstate, "tp", axis=1, tiled=True)
        widened = whole_rows.astype(jnp.float32)
        inv_rms = lax.rsqrt(jnp.mean(widened * widened, axis=-1, keepdims=True) + 1e-05)
        normed = (widened * inv_rms * gain_full).astype(jnp.bfloat16)
        projected = jnp.dot(normed, weight_flat, preferred_element_type=jnp.float32).reshape(
            rows_per, 2, kv_heads, HD
        )
        new_keys = rotate(projected[:, 0], positions).astype(jnp.bfloat16)
        new_values = projected[:, 1].astype(jnp.bfloat16)
        fresh_kv = jnp.stack(
            [new_keys.reshape(rows_per, kv_width), new_values.reshape(rows_per, kv_width)], axis=1
        )
        gathered = layer_pages[page_table]
        cached = jnp.swapaxes(gathered, 1, 2).reshape(per_batch, 2, CTX, kv_heads, HD)
        fresh_heads = fresh_kv.reshape(per_batch, S, 2, kv_heads, HD)
        query_heads = queries[0].reshape(per_batch, S, kv_heads, group_size, HD)
        score_old = jnp.einsum(
            "bskgd,btkd->bskgt", query_heads, cached[:, 0], preferred_element_type=jnp.float32
        ) * HD ** (-0.5)
        score_new = jnp.einsum(
            "bskgd,btkd->bskgt",
            query_heads,
            fresh_heads[:, :, 0],
            preferred_element_type=jnp.float32,
        ) * HD ** (-0.5)
        old_ok = key_pos[None, :] < lengths[:, None]
        score_old = jnp.where(old_ok[:, None, None, None, :], score_old, -jnp.inf)
        score_new = jnp.where(causal[None, :, None, None, :], score_new, -jnp.inf)
        row_max = jnp.maximum(jnp.max(score_old, axis=-1), jnp.max(score_new, axis=-1))[..., None]
        exp_old = jnp.exp(score_old - row_max)
        exp_new = jnp.exp(score_new - row_max)
        denominator = (jnp.sum(exp_old, axis=-1) + jnp.sum(exp_new, axis=-1))[..., None]
        weight_old = (exp_old / denominator).astype(jnp.bfloat16)
        weight_new = (exp_new / denominator).astype(jnp.bfloat16)
        mixed = jnp.einsum(
            "bskgt,btkd->bskgd", weight_old, cached[:, 1], preferred_element_type=jnp.float32
        )
        mixed = mixed + jnp.einsum(
            "bskgt,btkd->bskgd",
            weight_new,
            fresh_heads[:, :, 1],
            preferred_element_type=jnp.float32,
        )
        attended = mixed.reshape(per_batch, S, q_width).astype(jnp.bfloat16)
        outgoing = (
            jnp.zeros((req_count, batch_cap, S, q_width), jnp.bfloat16)
            .at[dest_all, slot_all]
            .set(attended)
        )
        rows_in = exchange(outgoing, "req", 0)
        sources = rows_in.shape[0]
        item_count = rows_in.shape[1]
        flat_rows = rows_in.reshape(sources * item_count * S, q_width)
        all_low = jnp.einsum(
            "nf,arf->nar", flat_rows, adapters_in, preferred_element_type=jnp.float32
        )
        picks_rows = jnp.broadcast_to(picks_in[:, :, None], (sources, item_count, S)).reshape(
            sources * item_count * S
        )
        one_hot = (picks_rows[:, None] == adapter_slots[None, :]).astype(jnp.float32)
        partial_low = jnp.sum(all_low * one_hot[:, :, None], axis=1)
        rank_low = jnp.sum(exchange(partial_low, "tp", 1, gather=True), axis=0).astype(jnp.bfloat16)
        spread = (rank_low.astype(jnp.float32)[:, None, :] * one_hot[:, :, None]).astype(
            jnp.bfloat16
        )
        deltas = jnp.dot(
            spread.reshape(sources * item_count * S, ADP_DEV * R),
            adapters_out,
            preferred_element_type=jnp.float32,
        ).astype(jnp.bfloat16)
        deltas = deltas.reshape(sources, item_count, S, width_loc)
        returned = exchange(deltas, "req", 2)
        delta_rows = returned[dest_all, slot_all].reshape(rows_per, width_loc)
        new_state = (hstate.astype(jnp.float32) + delta_rows.astype(jnp.float32)).astype(
            jnp.bfloat16
        )
        section_rows = jnp.where(active, new_state, section_rows)
        fresh_rows = jnp.where(active, fresh_kv, fresh_rows)
        if tick_id + 1 < section_count:
            carried = passed_along(new_state, "pipe", tick_id)

    patch = jnp.dot(
        tok_pick, fresh_rows.reshape(RQ * S, 2 * kv_width), preferred_element_type=jnp.float32
    ).astype(jnp.bfloat16)
    patch = jnp.swapaxes(patch.reshape(req_count * pair_cap, PAGE, 2, kv_width), 1, 2)
    sent_pages = jnp.where(tok_hit[:, None, :, None], patch, out_pages).reshape(
        req_count, pair_cap, 2, PAGE, kv_width
    )
    got_pages = exchange(sent_pages, "req", 3).reshape(req_count * pair_cap, 2, PAGE, kv_width)
    arrived = jnp.where(
        has_page[:, None, None, None], got_pages[page_src], jnp.zeros((), jnp.bfloat16)
    )
    return (section_rows[None], fresh_rows[None], arrived[None])


def solution(mesh):
    in_specs = (
        P("req", "tp"),
        P("pipe", "req", "tp"),
        P("pipe", None),
        P("pipe", None, None, "tp"),
        P("pipe", "req", None, "tp"),
        P("pipe", "req", None, "tp"),
        P("pipe", "req", None, None, "tp"),
        P("req"),
        P(),
        P("req", None),
        P("req"),
        P("req", None),
    )
    out_specs = (
        P("pipe", "req", "tp"),
        P("pipe", "req", None, "tp"),
        P("pipe", "req", None, None, "tp"),
    )
    return jax.shard_map(body, mesh=mesh, in_specs=in_specs, out_specs=out_specs, check_vma=False)
```

```python
import functools
import math

import jax
import jax.numpy as jnp
from jax import lax
from jax.experimental import pallas as pl
from jax.experimental.pallas import tpu as pltpu
from jax.sharding import PartitionSpec as P

D = 8192
HD = 128
R = 64
ADP_DEV = 4
RQ = 32
S = 4
MICRO = 2
PAGE = 64
MOVES = 16
RQ_MB = 16
CTX = 256


def passed_along(block, axis, source):
    return lax.ppermute(block, axis, [(source, source + 1)])


def exchange_kernel(axis, n, gather, gate, x_ref, o_ref, send_sem, recv_sem, local_sem):
    if gate is None:
        exchange_body(axis, n, gather, x_ref, o_ref, send_sem, recv_sem, local_sem)
    else:
        pl.when(lax.axis_index("pipe") == gate)(
            lambda: exchange_body(axis, n, gather, x_ref, o_ref, send_sem, recv_sem, local_sem)
        )


def exchange_body(axis, n, gather, x_ref, o_ref, send_sem, recv_sem, local_sem):
    me = lax.axis_index(axis)
    barrier = pltpu.get_barrier_semaphore()
    for j in range(1, n):
        pl.semaphore_signal(
            barrier, 1, device_id={axis: (me + j) % n}, device_id_type=pl.DeviceIdType.MESH
        )
    pl.semaphore_wait(barrier, n - 1)
    copies = []
    for j in range(1, n):
        peer = (me + j) % n
        copy = pltpu.make_async_remote_copy(
            src_ref=x_ref if gather else x_ref.at[peer],
            dst_ref=o_ref.at[me],
            send_sem=send_sem.at[j],
            recv_sem=recv_sem.at[j],
            device_id={axis: peer},
            device_id_type=pl.DeviceIdType.MESH,
        )
        copy.start()
        copies.append(copy)
    local = pltpu.make_async_copy(x_ref if gather else x_ref.at[me], o_ref.at[me], local_sem)
    local.start()
    local.wait()
    for copy in copies:
        copy.wait()


def exchange(x, axis, collective_id, gather=False, gate=None):
    n = lax.axis_size(axis)
    out_shape = (n,) + x.shape if gather else x.shape
    return pl.pallas_call(
        functools.partial(exchange_kernel, axis, n, gather, gate),
        out_shape=jax.ShapeDtypeStruct(out_shape, x.dtype),
        in_specs=[pl.BlockSpec(memory_space=pl.ANY)],
        out_specs=pl.BlockSpec(memory_space=pl.ANY),
        scratch_shapes=[
            pltpu.SemaphoreType.DMA((n,)),
            pltpu.SemaphoreType.DMA((n,)),
            pltpu.SemaphoreType.DMA(()),
        ],
        compiler_params=pltpu.CompilerParams(collective_id=collective_id, has_side_effects=True),
    )(x)


def rotate(key_vecs, positions):
    half_dim = key_vecs.shape[-1] // 2
    inv_freq = jnp.exp(
        -math.log(500000.0) * (2.0 * jnp.arange(half_dim, dtype=jnp.float32) / key_vecs.shape[-1])
    )
    angles = positions.astype(jnp.float32)[..., None, None] * inv_freq
    cos_vals = jnp.cos(angles)
    sin_vals = jnp.sin(angles)
    front_half = key_vecs[..., :half_dim]
    back_half = key_vecs[..., half_dim:]
    return jnp.concatenate(
        [
            front_half * cos_vals - back_half * sin_vals,
            back_half * cos_vals + front_half * sin_vals,
        ],
        axis=-1,
    )


def body(
    hidden,
    queries,
    norm_gain,
    kv_weight,
    adapter_in,
    adapter_out,
    kv_pages,
    adapter_ids,
    owner_rows,
    page_table,
    lengths,
    moves,
):
    section_count = lax.axis_size("pipe")
    req_count = lax.axis_size("req")
    section_id = lax.axis_index("pipe")
    my_req = lax.axis_index("req")
    width_loc = hidden.shape[1]
    q_width = queries.shape[2]
    kv_width = kv_weight.shape[3]
    kv_heads = kv_width // HD
    group_size = q_width // HD // kv_heads
    batches = 1
    per_batch = RQ // batches
    rows_per = per_batch * S
    block_cap = min(RQ_MB, max(2, 2 * RQ_MB // req_count))
    batch_cap = block_cap * (MICRO // batches)
    pair_cap = (MOVES + req_count - 2) // (req_count - 1)
    free_slots = (req_count - 1) * pair_cap
    token_ids = jnp.arange(S, dtype=jnp.int32)
    store_rows = owner_rows[adapter_ids]
    dest_all = store_rows // ADP_DEV
    pick_all = store_rows % ADP_DEV
    req_ids = jnp.arange(RQ, dtype=jnp.int32)
    earlier = (
        (req_ids[None, :] < req_ids[:, None])
        & (req_ids[None, :] // per_batch == req_ids[:, None] // per_batch)
        & (dest_all[None, :] == dest_all[:, None])
    )
    slot_all = jnp.sum(earlier.astype(jnp.int32), axis=1)
    positions = (lengths[:, None] + token_ids[None, :]).reshape(RQ * S)
    gain_full = norm_gain[0].astype(jnp.float32)
    weight_flat = kv_weight[0].reshape(D, 2 * kv_width)
    layer_pages = kv_pages[0]
    adapters_in = adapter_in[0]
    adapters_out = adapter_out[0].reshape(ADP_DEV * R, width_loc)
    key_pos = jnp.arange(CTX, dtype=jnp.int32)
    causal = token_ids[None, :] <= token_ids[:, None]
    adapter_slots = jnp.arange(ADP_DEV, dtype=jnp.int32)
    move_ids = jnp.arange(MOVES, dtype=jnp.int32)
    move_dest = moves[:, 0]
    move_slot = jnp.sum(
        (
            (move_ids[None, :] < move_ids[:, None]) & (move_dest[None, :] == move_dest[:, None])
        ).astype(jnp.int32),
        axis=1,
    )
    picks_out = jnp.zeros((req_count, batch_cap), jnp.int32).at[dest_all, slot_all].set(pick_all)
    spots_out = jnp.full((req_count, pair_cap), -1, jnp.int32).at[move_dest, move_slot].set(moves[:, 2])
    ints_in = lax.all_to_all(
        jnp.concatenate([picks_out, spots_out], axis=1), "req", split_axis=0, concat_axis=0, tiled=True
    )
    picks_in = ints_in[:, :batch_cap]
    spots_in = ints_in[:, batch_cap:].reshape(req_count * pair_cap)
    spot_match = spots_in[None, :] == jnp.arange(free_slots, dtype=jnp.int32)[:, None]
    has_page = jnp.any(spot_match, axis=1)
    page_src = jnp.argmax(spot_match, axis=1)
    box_ids = jnp.arange(req_count * pair_cap, dtype=jnp.int32)
    box_match = (move_dest * pair_cap + move_slot)[None, :] == box_ids[:, None]
    box_move = jnp.argmax(box_match, axis=1)
    box_used = jnp.any(box_match, axis=1)
    box_page = jnp.where(box_used, moves[box_move, 1], -1)
    out_pages = jnp.where(
        box_used[:, None, None, None], layer_pages[moves[box_move, 1]], jnp.zeros((), jnp.bfloat16)
    )
    page_slot = jnp.take_along_axis(page_table, (positions // PAGE).reshape(RQ, S), axis=1).reshape(
        RQ * S
    )
    spot_ids = jnp.arange(req_count * pair_cap * PAGE, dtype=jnp.int32)
    tok_match = (
        (page_slot[None, :] == box_page[spot_ids // PAGE][:, None])
        & ((positions % PAGE)[None, :] == (spot_ids % PAGE)[:, None])
    )
    tok_pick = tok_match.astype(jnp.bfloat16)
    tok_hit = jnp.any(tok_match, axis=1).reshape(req_count * pair_cap, PAGE)
    tp_count = lax.axis_size("tp")
    my_tp = lax.axis_index("tp")
    gain_own = lax.dynamic_slice_in_dim(gain_full, my_tp * width_loc, width_loc)
    weight_own = kv_weight[0].reshape(D, 2 * kv_width)
    relative_rows = [lax.dynamic_slice_in_dim(weight_own, my_tp * width_loc, width_loc, axis=0)]
    later = [(p * tp_count + t) for p in range(1, section_count) for t in range(tp_count)]
    for shift in range(1, tp_count):
        outgoing_rows = lax.dynamic_slice_in_dim(
            weight_own, ((my_tp + shift) % tp_count) * width_loc, width_loc, axis=0
        )
        route = [(i, i - i % tp_count + (i % tp_count + shift) % tp_count) for i in later]
        relative_rows.append(lax.ppermute(outgoing_rows, ("pipe", "tp"), route))
    weight_rows = jnp.concatenate(relative_rows, axis=1)
    block_order = (my_tp - jnp.arange(tp_count, dtype=jnp.int32)) % tp_count
    carried = jnp.zeros((rows_per, width_loc), jnp.bfloat16)
    section_rows = jnp.zeros((RQ * S, width_loc), jnp.bfloat16)
    fresh_rows = jnp.zeros((RQ * S, 2, kv_width), jnp.bfloat16)
    for tick_id in range(batches + section_count - 1):
        offset_batch = tick_id - section_id
        active = (offset_batch >= 0) & (offset_batch < batches)
        if tick_id == 0:
            hstate = hidden
            whole_rows = lax.all_gather(hstate, "tp", axis=1, tiled=True)
            widened = whole_rows.astype(jnp.float32)
            inv_rms = lax.rsqrt(jnp.mean(widened * widened, axis=-1, keepdims=True) + 1e-05)
            normed = (widened * inv_rms * gain_full).astype(jnp.bfloat16)
            projected = jnp.dot(normed, weight_flat, preferred_element_type=jnp.float32)
        else:
            hstate = carried
            widened = hstate.astype(jnp.float32)
            scaled = (widened * gain_own).astype(jnp.bfloat16)
            part_rel = jnp.dot(scaled, weight_rows, preferred_element_type=jnp.float32).reshape(
                rows_per, tp_count, 2 * kv_width
            )
            part_abs = jnp.swapaxes(jnp.take(part_rel, block_order, axis=1), 0, 1)
            sumsq = jnp.sum(widened * widened, axis=-1)
            sumsq_rows = jnp.zeros((tp_count, 8, 2 * kv_width), jnp.float32).at[:, 0, :rows_per].set(
                jnp.broadcast_to(sumsq, (tp_count, rows_per))
            )
            got = exchange(jnp.concatenate([part_abs, sumsq_rows], axis=1), "tp", 10 + tick_id)
            got = jnp.sum(got, axis=0)
            inv_rms = lax.rsqrt(got[rows_per, :rows_per] / D + 1e-05)
            projected = got[:rows_per] * inv_rms[:, None]
        projected = projected.reshape(rows_per, 2, kv_heads, HD)
        new_keys = rotate(projected[:, 0], positions).astype(jnp.bfloat16)
        new_values = projected[:, 1].astype(jnp.bfloat16)
        fresh_kv = jnp.stack(
            [new_keys.reshape(rows_per, kv_width), new_values.reshape(rows_per, kv_width)], axis=1
        )
        gathered = layer_pages[page_table]
        cached = jnp.swapaxes(gathered, 1, 2).reshape(per_batch, 2, CTX, kv_heads, HD)
        fresh_heads = fresh_kv.reshape(per_batch, S, 2, kv_heads, HD)
        query_heads = queries[0].reshape(per_batch, S, kv_heads, group_size, HD)
        score_old = jnp.einsum(
            "bskgd,btkd->bskgt", query_heads, cached[:, 0], preferred_element_type=jnp.float32
        ) * HD ** (-0.5)
        score_new = jnp.einsum(
            "bskgd,btkd->bskgt",
            query_heads,
            fresh_heads[:, :, 0],
            preferred_element_type=jnp.float32,
        ) * HD ** (-0.5)
        old_ok = key_pos[None, :] < lengths[:, None]
        score_old = jnp.where(old_ok[:, None, None, None, :], score_old, -jnp.inf)
        score_new = jnp.where(causal[None, :, None, None, :], score_new, -jnp.inf)
        row_max = jnp.maximum(jnp.max(score_old, axis=-1), jnp.max(score_new, axis=-1))[..., None]
        exp_old = jnp.exp(score_old - row_max)
        exp_new = jnp.exp(score_new - row_max)
        denominator = (jnp.sum(exp_old, axis=-1) + jnp.sum(exp_new, axis=-1))[..., None]
        weight_old = (exp_old / denominator).astype(jnp.bfloat16)
        weight_new = (exp_new / denominator).astype(jnp.bfloat16)
        mixed = jnp.einsum(
            "bskgt,btkd->bskgd", weight_old, cached[:, 1], preferred_element_type=jnp.float32
        )
        mixed = mixed + jnp.einsum(
            "bskgt,btkd->bskgd",
            weight_new,
            fresh_heads[:, :, 1],
            preferred_element_type=jnp.float32,
        )
        attended = mixed.reshape(per_batch, S, q_width).astype(jnp.bfloat16)
        outgoing = (
            jnp.zeros((req_count, batch_cap, S, q_width), jnp.bfloat16)
            .at[dest_all, slot_all]
            .set(attended)
        )
        rows_in = exchange(outgoing, "req", 0)
        sources = rows_in.shape[0]
        item_count = rows_in.shape[1]
        flat_rows = rows_in.reshape(sources * item_count * S, q_width)
        all_low = jnp.einsum(
            "nf,arf->nar", flat_rows, adapters_in, preferred_element_type=jnp.float32
        )
        picks_rows = jnp.broadcast_to(picks_in[:, :, None], (sources, item_count, S)).reshape(
            sources * item_count * S
        )
        one_hot = (picks_rows[:, None] == adapter_slots[None, :]).astype(jnp.float32)
        partial_low = jnp.sum(all_low * one_hot[:, :, None], axis=1)
        rank_low = jnp.sum(exchange(partial_low, "tp", 1, gather=True), axis=0).astype(jnp.bfloat16)
        spread = (rank_low.astype(jnp.float32)[:, None, :] * one_hot[:, :, None]).astype(
            jnp.bfloat16
        )
        deltas = jnp.dot(
            spread.reshape(sources * item_count * S, ADP_DEV * R),
            adapters_out,
            preferred_element_type=jnp.float32,
        ).astype(jnp.bfloat16)
        deltas = deltas.reshape(sources, item_count, S, width_loc)
        returned = exchange(deltas, "req", 2)
        delta_rows = returned[dest_all, slot_all].reshape(rows_per, width_loc)
        new_state = (hstate.astype(jnp.float32) + delta_rows.astype(jnp.float32)).astype(
            jnp.bfloat16
        )
        section_rows = jnp.where(active, new_state, section_rows)
        fresh_rows = jnp.where(active, fresh_kv, fresh_rows)
        if tick_id + 1 < section_count:
            carried = passed_along(new_state, "pipe", tick_id)

    patch = jnp.dot(
        tok_pick, fresh_rows.reshape(RQ * S, 2 * kv_width), preferred_element_type=jnp.float32
    ).astype(jnp.bfloat16)
    patch = jnp.swapaxes(patch.reshape(req_count * pair_cap, PAGE, 2, kv_width), 1, 2)
    sent_pages = jnp.where(tok_hit[:, None, :, None], patch, out_pages).reshape(
        req_count, pair_cap, 2, PAGE, kv_width
    )
    got_pages = exchange(sent_pages, "req", 3).reshape(req_count * pair_cap, 2, PAGE, kv_width)
    arrived = jnp.where(
        has_page[:, None, None, None], got_pages[page_src], jnp.zeros((), jnp.bfloat16)
    )
    return (section_rows[None], fresh_rows[None], arrived[None])


def solution(mesh):
    in_specs = (
        P("req", "tp"),
        P("pipe", "req", "tp"),
        P("pipe", None),
        P("pipe", None, None, "tp"),
        P("pipe", "req", None, "tp"),
        P("pipe", "req", None, "tp"),
        P("pipe", "req", None, None, "tp"),
        P("req"),
        P(),
        P("req", None),
        P("req"),
        P("req", None),
    )
    out_specs = (
        P("pipe", "req", "tp"),
        P("pipe", "req", None, "tp"),
        P("pipe", "req", None, None, "tp"),
    )
    return jax.shard_map(body, mesh=mesh, in_specs=in_specs, out_specs=out_specs, check_vma=False)
```

```python
import functools
import math

import jax
import jax.numpy as jnp
from jax import lax
from jax.experimental import pallas as pl
from jax.experimental.pallas import tpu as pltpu
from jax.sharding import PartitionSpec as P

D = 8192
HD = 128
R = 64
ADP_DEV = 4
RQ = 32
S = 4
MICRO = 2
PAGE = 64
MOVES = 16
RQ_MB = 16
CTX = 256


def passed_along(block, axis, source):
    return lax.ppermute(block, axis, [(source, source + 1)])


def exchange_kernel(axis, n, gather, gate, x_ref, o_ref, send_sem, recv_sem, local_sem):
    if gate is None:
        exchange_body(axis, n, gather, x_ref, o_ref, send_sem, recv_sem, local_sem)
    else:
        pl.when(lax.axis_index("pipe") == gate)(
            lambda: exchange_body(axis, n, gather, x_ref, o_ref, send_sem, recv_sem, local_sem)
        )


def exchange_body(axis, n, gather, x_ref, o_ref, send_sem, recv_sem, local_sem):
    me = lax.axis_index(axis)
    barrier = pltpu.get_barrier_semaphore()
    for j in range(1, n):
        pl.semaphore_signal(
            barrier, 1, device_id={axis: (me + j) % n}, device_id_type=pl.DeviceIdType.MESH
        )
    pl.semaphore_wait(barrier, n - 1)
    copies = []
    for j in range(1, n):
        peer = (me + j) % n
        copy = pltpu.make_async_remote_copy(
            src_ref=x_ref if gather else x_ref.at[peer],
            dst_ref=o_ref.at[me],
            send_sem=send_sem.at[j],
            recv_sem=recv_sem.at[j],
            device_id={axis: peer},
            device_id_type=pl.DeviceIdType.MESH,
        )
        copy.start()
        copies.append(copy)
    local = pltpu.make_async_copy(x_ref if gather else x_ref.at[me], o_ref.at[me], local_sem)
    local.start()
    local.wait()
    for copy in copies:
        copy.wait()


def exchange(x, axis, collective_id, gather=False, gate=None):
    n = lax.axis_size(axis)
    out_shape = (n,) + x.shape if gather else x.shape
    return pl.pallas_call(
        functools.partial(exchange_kernel, axis, n, gather, gate),
        out_shape=jax.ShapeDtypeStruct(out_shape, x.dtype),
        in_specs=[pl.BlockSpec(memory_space=pl.ANY)],
        out_specs=pl.BlockSpec(memory_space=pl.ANY),
        scratch_shapes=[
            pltpu.SemaphoreType.DMA((n,)),
            pltpu.SemaphoreType.DMA((n,)),
            pltpu.SemaphoreType.DMA(()),
        ],
        compiler_params=pltpu.CompilerParams(collective_id=collective_id, has_side_effects=True),
    )(x)


def rotate(key_vecs, positions):
    half_dim = key_vecs.shape[-1] // 2
    inv_freq = jnp.exp(
        -math.log(500000.0) * (2.0 * jnp.arange(half_dim, dtype=jnp.float32) / key_vecs.shape[-1])
    )
    angles = positions.astype(jnp.float32)[..., None, None] * inv_freq
    cos_vals = jnp.cos(angles)
    sin_vals = jnp.sin(angles)
    front_half = key_vecs[..., :half_dim]
    back_half = key_vecs[..., half_dim:]
    return jnp.concatenate(
        [
            front_half * cos_vals - back_half * sin_vals,
            back_half * cos_vals + front_half * sin_vals,
        ],
        axis=-1,
    )


def body(
    hidden,
    queries,
    norm_gain,
    kv_weight,
    adapter_in,
    adapter_out,
    kv_pages,
    adapter_ids,
    owner_rows,
    page_table,
    lengths,
    moves,
):
    section_count = lax.axis_size("pipe")
    req_count = lax.axis_size("req")
    section_id = lax.axis_index("pipe")
    my_req = lax.axis_index("req")
    width_loc = hidden.shape[1]
    q_width = queries.shape[2]
    kv_width = kv_weight.shape[3]
    kv_heads = kv_width // HD
    group_size = q_width // HD // kv_heads
    batches = 1
    per_batch = RQ // batches
    rows_per = per_batch * S
    block_cap = min(RQ_MB, max(2, 2 * RQ_MB // req_count))
    batch_cap = block_cap * (MICRO // batches)
    pair_cap = (MOVES + req_count - 2) // (req_count - 1)
    free_slots = (req_count - 1) * pair_cap
    token_ids = jnp.arange(S, dtype=jnp.int32)
    store_rows = owner_rows[adapter_ids]
    dest_all = store_rows // ADP_DEV
    pick_all = store_rows % ADP_DEV
    req_ids = jnp.arange(RQ, dtype=jnp.int32)
    earlier = (
        (req_ids[None, :] < req_ids[:, None])
        & (req_ids[None, :] // per_batch == req_ids[:, None] // per_batch)
        & (dest_all[None, :] == dest_all[:, None])
    )
    slot_all = jnp.sum(earlier.astype(jnp.int32), axis=1)
    positions = (lengths[:, None] + token_ids[None, :]).reshape(RQ * S)
    gain_full = norm_gain[0].astype(jnp.float32)
    weight_flat = kv_weight[0].reshape(D, 2 * kv_width)
    layer_pages = kv_pages[0]
    adapters_in = adapter_in[0]
    adapters_out = adapter_out[0].reshape(ADP_DEV * R, width_loc)
    key_pos = jnp.arange(CTX, dtype=jnp.int32)
    causal = token_ids[None, :] <= token_ids[:, None]
    adapter_slots = jnp.arange(ADP_DEV, dtype=jnp.int32)
    move_ids = jnp.arange(MOVES, dtype=jnp.int32)
    move_dest = moves[:, 0]
    move_slot = jnp.sum(
        (
            (move_ids[None, :] < move_ids[:, None]) & (move_dest[None, :] == move_dest[:, None])
        ).astype(jnp.int32),
        axis=1,
    )
    picks_out = jnp.zeros((req_count, batch_cap), jnp.int32).at[dest_all, slot_all].set(pick_all)
    spots_out = jnp.full((req_count, pair_cap), -1, jnp.int32).at[move_dest, move_slot].set(moves[:, 2])
    ints_in = lax.all_to_all(
        jnp.concatenate([picks_out, spots_out], axis=1), "req", split_axis=0, concat_axis=0, tiled=True
    )
    picks_in = ints_in[:, :batch_cap]
    spots_in = ints_in[:, batch_cap:].reshape(req_count * pair_cap)
    spot_match = spots_in[None, :] == jnp.arange(free_slots, dtype=jnp.int32)[:, None]
    has_page = jnp.any(spot_match, axis=1)
    page_src = jnp.argmax(spot_match, axis=1)
    box_ids = jnp.arange(req_count * pair_cap, dtype=jnp.int32)
    box_match = (move_dest * pair_cap + move_slot)[None, :] == box_ids[:, None]
    box_move = jnp.argmax(box_match, axis=1)
    box_used = jnp.any(box_match, axis=1)
    box_page = jnp.where(box_used, moves[box_move, 1], -1)
    box_pick = (box_page[:, None] == jnp.arange(layer_pages.shape[0], dtype=jnp.int32)[None, :]).astype(
        jnp.bfloat16
    )
    land_pick = (spot_match & has_page[:, None]).astype(jnp.bfloat16)
    box_count = req_count * pair_cap

    def build_pages(fresh):
        base = jnp.dot(
            box_pick, layer_pages.reshape(layer_pages.shape[0], -1), preferred_element_type=jnp.float32
        ).astype(jnp.bfloat16).reshape(box_count, 2, PAGE, kv_width)
        patch = jnp.dot(
            tok_pick, fresh.reshape(RQ * S, 2 * kv_width), preferred_element_type=jnp.float32
        ).astype(jnp.bfloat16)
        patch = jnp.swapaxes(patch.reshape(box_count, PAGE, 2, kv_width), 1, 2)
        return jnp.where(tok_hit[:, None, :, None], patch, base).reshape(
            req_count, pair_cap, 2, PAGE, kv_width
        )

    def no_pages(fresh):
        return jnp.zeros((req_count, pair_cap, 2, PAGE, kv_width), jnp.bfloat16)

    arrived = jnp.zeros((free_slots, 2, PAGE, kv_width), jnp.bfloat16)
    page_slot = jnp.take_along_axis(page_table, (positions // PAGE).reshape(RQ, S), axis=1).reshape(
        RQ * S
    )
    spot_ids = jnp.arange(req_count * pair_cap * PAGE, dtype=jnp.int32)
    tok_match = (
        (page_slot[None, :] == box_page[spot_ids // PAGE][:, None])
        & ((positions % PAGE)[None, :] == (spot_ids % PAGE)[:, None])
    )
    tok_pick = tok_match.astype(jnp.bfloat16)
    tok_hit = jnp.any(tok_match, axis=1).reshape(req_count * pair_cap, PAGE)
    tp_count = lax.axis_size("tp")
    my_tp = lax.axis_index("tp")
    gain_own = lax.dynamic_slice_in_dim(gain_full, my_tp * width_loc, width_loc)
    weight_own = kv_weight[0].reshape(D, 2 * kv_width)
    relative_rows = [lax.dynamic_slice_in_dim(weight_own, my_tp * width_loc, width_loc, axis=0)]
    later = [(p * tp_count + t) for p in range(1, section_count) for t in range(tp_count)]
    for shift in range(1, tp_count):
        outgoing_rows = lax.dynamic_slice_in_dim(
            weight_own, ((my_tp + shift) % tp_count) * width_loc, width_loc, axis=0
        )
        route = [(i, i - i % tp_count + (i % tp_count + shift) % tp_count) for i in later]
        relative_rows.append(lax.ppermute(outgoing_rows, ("pipe", "tp"), route))
    weight_rows = jnp.concatenate(relative_rows, axis=1)
    block_order = (my_tp - jnp.arange(tp_count, dtype=jnp.int32)) % tp_count
    carried = jnp.zeros((rows_per, width_loc), jnp.bfloat16)
    section_rows = jnp.zeros((RQ * S, width_loc), jnp.bfloat16)
    fresh_rows = jnp.zeros((RQ * S, 2, kv_width), jnp.bfloat16)
    for tick_id in range(batches + section_count - 1):
        offset_batch = tick_id - section_id
        active = (offset_batch >= 0) & (offset_batch < batches)
        if tick_id == 0:
            hstate = hidden
            whole_rows = lax.all_gather(hstate, "tp", axis=1, tiled=True)
            widened = whole_rows.astype(jnp.float32)
            inv_rms = lax.rsqrt(jnp.mean(widened * widened, axis=-1, keepdims=True) + 1e-05)
            normed = (widened * inv_rms * gain_full).astype(jnp.bfloat16)
            projected = jnp.dot(normed, weight_flat, preferred_element_type=jnp.float32)
        else:
            hstate = carried
            widened = hstate.astype(jnp.float32)
            scaled = (widened * gain_own).astype(jnp.bfloat16)
            part_rel = jnp.dot(scaled, weight_rows, preferred_element_type=jnp.float32).reshape(
                rows_per, tp_count, 2 * kv_width
            )
            part_abs = jnp.swapaxes(jnp.take(part_rel, block_order, axis=1), 0, 1)
            sumsq = jnp.sum(widened * widened, axis=-1)
            sumsq_rows = jnp.zeros((tp_count, 8, 2 * kv_width), jnp.float32).at[:, 0, :rows_per].set(
                jnp.broadcast_to(sumsq, (tp_count, rows_per))
            )
            got = exchange(
                jnp.concatenate([part_abs, sumsq_rows], axis=1), "tp", 10 + tick_id, gate=tick_id
            )
            got = jnp.sum(got, axis=0)
            inv_rms = lax.rsqrt(got[rows_per, :rows_per] / D + 1e-05)
            projected = got[:rows_per] * inv_rms[:, None]
        projected = projected.reshape(rows_per, 2, kv_heads, HD)
        new_keys = rotate(projected[:, 0], positions).astype(jnp.bfloat16)
        new_values = projected[:, 1].astype(jnp.bfloat16)
        fresh_kv = jnp.stack(
            [new_keys.reshape(rows_per, kv_width), new_values.reshape(rows_per, kv_width)], axis=1
        )
        gathered = layer_pages[page_table]
        cached = jnp.swapaxes(gathered, 1, 2).reshape(per_batch, 2, CTX, kv_heads, HD)
        fresh_heads = fresh_kv.reshape(per_batch, S, 2, kv_heads, HD)
        query_heads = queries[0].reshape(per_batch, S, kv_heads, group_size, HD)
        score_old = jnp.einsum(
            "bskgd,btkd->bskgt", query_heads, cached[:, 0], preferred_element_type=jnp.float32
        ) * HD ** (-0.5)
        score_new = jnp.einsum(
            "bskgd,btkd->bskgt",
            query_heads,
            fresh_heads[:, :, 0],
            preferred_element_type=jnp.float32,
        ) * HD ** (-0.5)
        old_ok = key_pos[None, :] < lengths[:, None]
        score_old = jnp.where(old_ok[:, None, None, None, :], score_old, -jnp.inf)
        score_new = jnp.where(causal[None, :, None, None, :], score_new, -jnp.inf)
        row_max = jnp.maximum(jnp.max(score_old, axis=-1), jnp.max(score_new, axis=-1))[..., None]
        exp_old = jnp.exp(score_old - row_max)
        exp_new = jnp.exp(score_new - row_max)
        denominator = (jnp.sum(exp_old, axis=-1) + jnp.sum(exp_new, axis=-1))[..., None]
        weight_old = (exp_old / denominator).astype(jnp.bfloat16)
        weight_new = (exp_new / denominator).astype(jnp.bfloat16)
        mixed = jnp.einsum(
            "bskgt,btkd->bskgd", weight_old, cached[:, 1], preferred_element_type=jnp.float32
        )
        mixed = mixed + jnp.einsum(
            "bskgt,btkd->bskgd",
            weight_new,
            fresh_heads[:, :, 1],
            preferred_element_type=jnp.float32,
        )
        attended = mixed.reshape(per_batch, S, q_width).astype(jnp.bfloat16)
        outgoing = (
            jnp.zeros((req_count, batch_cap, S, q_width), jnp.bfloat16)
            .at[dest_all, slot_all]
            .set(attended)
        )
        rows_in = exchange(outgoing, "req", 20 + tick_id, gate=tick_id)
        sources = rows_in.shape[0]
        item_count = rows_in.shape[1]
        flat_rows = rows_in.reshape(sources * item_count * S, q_width)
        all_low = jnp.einsum(
            "nf,arf->nar", flat_rows, adapters_in, preferred_element_type=jnp.float32
        )
        picks_rows = jnp.broadcast_to(picks_in[:, :, None], (sources, item_count, S)).reshape(
            sources * item_count * S
        )
        one_hot = (picks_rows[:, None] == adapter_slots[None, :]).astype(jnp.float32)
        partial_low = jnp.sum(all_low * one_hot[:, :, None], axis=1)
        rank_low = jnp.sum(exchange(partial_low, "tp", 30 + tick_id, gather=True, gate=tick_id), axis=0).astype(jnp.bfloat16)
        spread = (rank_low.astype(jnp.float32)[:, None, :] * one_hot[:, :, None]).astype(
            jnp.bfloat16
        )
        deltas = jnp.dot(
            spread.reshape(sources * item_count * S, ADP_DEV * R),
            adapters_out,
            preferred_element_type=jnp.float32,
        ).astype(jnp.bfloat16)
        deltas = deltas.reshape(sources, item_count, S, width_loc)
        returned = exchange(deltas, "req", 40 + tick_id, gate=tick_id)
        delta_rows = returned[dest_all, slot_all].reshape(rows_per, width_loc)
        new_state = (hstate.astype(jnp.float32) + delta_rows.astype(jnp.float32)).astype(
            jnp.bfloat16
        )
        section_rows = jnp.where(active, new_state, section_rows)
        fresh_rows = jnp.where(active, fresh_kv, fresh_rows)
        if tick_id + 1 < section_count:
            carried = passed_along(new_state, "pipe", tick_id)
        sent_pages = lax.cond(section_id == tick_id, build_pages, no_pages, fresh_kv)
        got_pages = exchange(sent_pages, "req", 50 + tick_id, gate=tick_id)
        landed = jnp.dot(
            land_pick, got_pages.reshape(box_count, -1), preferred_element_type=jnp.float32
        ).astype(jnp.bfloat16)
        arrived = jnp.where(
            section_id == tick_id, landed.reshape(free_slots, 2, PAGE, kv_width), arrived
        )

    return (section_rows[None], fresh_rows[None], arrived[None])


def solution(mesh):
    in_specs = (
        P("req", "tp"),
        P("pipe", "req", "tp"),
        P("pipe", None),
        P("pipe", None, None, "tp"),
        P("pipe", "req", None, "tp"),
        P("pipe", "req", None, "tp"),
        P("pipe", "req", None, None, "tp"),
        P("req"),
        P(),
        P("req", None),
        P("req"),
        P("req", None),
    )
    out_specs = (
        P("pipe", "req", "tp"),
        P("pipe", "req", None, "tp"),
        P("pipe", "req", None, None, "tp"),
    )
    return jax.shard_map(body, mesh=mesh, in_specs=in_specs, out_specs=out_specs, check_vma=False)
```

```python
import functools
import math

import jax
import jax.numpy as jnp
from jax import lax
from jax.experimental import pallas as pl
from jax.experimental.pallas import tpu as pltpu
from jax.sharding import PartitionSpec as P

D = 8192
HD = 128
R = 64
ADP_DEV = 4
RQ = 32
S = 4
MICRO = 2
PAGE = 64
MOVES = 16
RQ_MB = 16
CTX = 256


def passed_along(block, axis, source):
    return lax.ppermute(block, axis, [(source, source + 1)])


def exchange_kernel(axis, n, gather, gate, x_ref, o_ref, send_sem, recv_sem, local_sem):
    if gate is None:
        exchange_body(axis, n, gather, x_ref, o_ref, send_sem, recv_sem, local_sem)
    else:
        pl.when(lax.axis_index("pipe") == gate)(
            lambda: exchange_body(axis, n, gather, x_ref, o_ref, send_sem, recv_sem, local_sem)
        )


def exchange_body(axis, n, gather, x_ref, o_ref, send_sem, recv_sem, local_sem):
    me = lax.axis_index(axis)
    barrier = pltpu.get_barrier_semaphore()
    for j in range(1, n):
        pl.semaphore_signal(
            barrier, 1, device_id={axis: (me + j) % n}, device_id_type=pl.DeviceIdType.MESH
        )
    pl.semaphore_wait(barrier, n - 1)
    copies = []
    for j in range(1, n):
        peer = (me + j) % n
        copy = pltpu.make_async_remote_copy(
            src_ref=x_ref if gather else x_ref.at[peer],
            dst_ref=o_ref.at[me],
            send_sem=send_sem.at[j],
            recv_sem=recv_sem.at[j],
            device_id={axis: peer},
            device_id_type=pl.DeviceIdType.MESH,
        )
        copy.start()
        copies.append(copy)
    local = pltpu.make_async_copy(x_ref if gather else x_ref.at[me], o_ref.at[me], local_sem)
    local.start()
    local.wait()
    for copy in copies:
        copy.wait()


def exchange(x, axis, collective_id, gather=False, gate=None):
    n = lax.axis_size(axis)
    out_shape = (n,) + x.shape if gather else x.shape
    return pl.pallas_call(
        functools.partial(exchange_kernel, axis, n, gather, gate),
        out_shape=jax.ShapeDtypeStruct(out_shape, x.dtype),
        in_specs=[pl.BlockSpec(memory_space=pl.ANY)],
        out_specs=pl.BlockSpec(memory_space=pl.ANY),
        scratch_shapes=[
            pltpu.SemaphoreType.DMA((n,)),
            pltpu.SemaphoreType.DMA((n,)),
            pltpu.SemaphoreType.DMA(()),
        ],
        compiler_params=pltpu.CompilerParams(collective_id=collective_id, has_side_effects=True),
    )(x)


def rotate(key_vecs, positions):
    half_dim = key_vecs.shape[-1] // 2
    inv_freq = jnp.exp(
        -math.log(500000.0) * (2.0 * jnp.arange(half_dim, dtype=jnp.float32) / key_vecs.shape[-1])
    )
    angles = positions.astype(jnp.float32)[..., None, None] * inv_freq
    cos_vals = jnp.cos(angles)
    sin_vals = jnp.sin(angles)
    front_half = key_vecs[..., :half_dim]
    back_half = key_vecs[..., half_dim:]
    return jnp.concatenate(
        [
            front_half * cos_vals - back_half * sin_vals,
            back_half * cos_vals + front_half * sin_vals,
        ],
        axis=-1,
    )


def body(
    hidden,
    queries,
    norm_gain,
    kv_weight,
    adapter_in,
    adapter_out,
    kv_pages,
    adapter_ids,
    owner_rows,
    page_table,
    lengths,
    moves,
):
    section_count = lax.axis_size("pipe")
    req_count = lax.axis_size("req")
    section_id = lax.axis_index("pipe")
    my_req = lax.axis_index("req")
    width_loc = hidden.shape[1]
    q_width = queries.shape[2]
    kv_width = kv_weight.shape[3]
    kv_heads = kv_width // HD
    group_size = q_width // HD // kv_heads
    batches = 1
    per_batch = RQ // batches
    rows_per = per_batch * S
    block_cap = min(RQ_MB, max(2, 2 * RQ_MB // req_count))
    batch_cap = block_cap * (MICRO // batches)
    pair_cap = (MOVES + req_count - 2) // (req_count - 1)
    free_slots = (req_count - 1) * pair_cap
    token_ids = jnp.arange(S, dtype=jnp.int32)
    store_rows = owner_rows[adapter_ids]
    dest_all = store_rows // ADP_DEV
    pick_all = store_rows % ADP_DEV
    req_ids = jnp.arange(RQ, dtype=jnp.int32)
    earlier = (
        (req_ids[None, :] < req_ids[:, None])
        & (req_ids[None, :] // per_batch == req_ids[:, None] // per_batch)
        & (dest_all[None, :] == dest_all[:, None])
    )
    slot_all = jnp.sum(earlier.astype(jnp.int32), axis=1)
    positions = (lengths[:, None] + token_ids[None, :]).reshape(RQ * S)
    gain_full = norm_gain[0].astype(jnp.float32)
    weight_flat = kv_weight[0].reshape(D, 2 * kv_width)
    layer_pages = kv_pages[0]
    adapters_in = adapter_in[0]
    adapters_out = adapter_out[0].reshape(ADP_DEV * R, width_loc)
    key_pos = jnp.arange(CTX, dtype=jnp.int32)
    causal = token_ids[None, :] <= token_ids[:, None]
    adapter_slots = jnp.arange(ADP_DEV, dtype=jnp.int32)
    move_ids = jnp.arange(MOVES, dtype=jnp.int32)
    move_dest = moves[:, 0]
    move_slot = jnp.sum(
        (
            (move_ids[None, :] < move_ids[:, None]) & (move_dest[None, :] == move_dest[:, None])
        ).astype(jnp.int32),
        axis=1,
    )
    picks_out = jnp.zeros((req_count, batch_cap), jnp.int32).at[dest_all, slot_all].set(pick_all)
    spots_out = jnp.full((req_count, pair_cap), -1, jnp.int32).at[move_dest, move_slot].set(moves[:, 2])
    ints_in = lax.all_to_all(
        jnp.concatenate([picks_out, spots_out], axis=1), "req", split_axis=0, concat_axis=0, tiled=True
    )
    picks_in = ints_in[:, :batch_cap]
    spots_in = ints_in[:, batch_cap:].reshape(req_count * pair_cap)
    spot_match = spots_in[None, :] == jnp.arange(free_slots, dtype=jnp.int32)[:, None]
    has_page = jnp.any(spot_match, axis=1)
    page_src = jnp.argmax(spot_match, axis=1)
    box_ids = jnp.arange(req_count * pair_cap, dtype=jnp.int32)
    box_match = (move_dest * pair_cap + move_slot)[None, :] == box_ids[:, None]
    box_move = jnp.argmax(box_match, axis=1)
    box_used = jnp.any(box_match, axis=1)
    box_page = jnp.where(box_used, moves[box_move, 1], -1)
    box_pick = (box_page[:, None] == jnp.arange(layer_pages.shape[0], dtype=jnp.int32)[None, :]).astype(
        jnp.bfloat16
    )
    land_pick = (spot_match & has_page[:, None]).astype(jnp.bfloat16)
    box_count = req_count * pair_cap

    def build_pages(fresh):
        spot_ids = jnp.arange(req_count * pair_cap * PAGE, dtype=jnp.int32)
        tok_match = tok_spot[None, :] == spot_ids[:, None]
        tok_pick = tok_match.astype(jnp.bfloat16)
        tok_hit = jnp.any(tok_match, axis=1).reshape(req_count * pair_cap, PAGE)
        base = jnp.dot(
            box_pick, layer_pages.reshape(layer_pages.shape[0], -1), preferred_element_type=jnp.float32
        ).astype(jnp.bfloat16).reshape(box_count, 2, PAGE, kv_width)
        patch = jnp.dot(
            tok_pick, fresh.reshape(RQ * S, 2 * kv_width), preferred_element_type=jnp.float32
        ).astype(jnp.bfloat16)
        patch = jnp.swapaxes(patch.reshape(box_count, PAGE, 2, kv_width), 1, 2)
        return jnp.where(tok_hit[:, None, :, None], patch, base).reshape(
            req_count, pair_cap, 2, PAGE, kv_width
        )

    def no_pages(fresh):
        return jnp.zeros((req_count, pair_cap, 2, PAGE, kv_width), jnp.bfloat16)

    arrived = jnp.zeros((free_slots, 2, PAGE, kv_width), jnp.bfloat16)
    page_slot = jnp.take_along_axis(page_table, (positions // PAGE).reshape(RQ, S), axis=1).reshape(
        RQ * S
    )
    tok_in_box = page_slot[:, None] == box_page[None, :]
    tok_spot = jnp.where(
        jnp.any(tok_in_box, axis=1),
        jnp.argmax(tok_in_box, axis=1).astype(jnp.int32) * PAGE + positions % PAGE,
        -1,
    )
    tp_count = lax.axis_size("tp")
    my_tp = lax.axis_index("tp")
    gain_own = lax.dynamic_slice_in_dim(gain_full, my_tp * width_loc, width_loc)
    weight_own = kv_weight[0].reshape(D, 2 * kv_width)
    relative_rows = [lax.dynamic_slice_in_dim(weight_own, my_tp * width_loc, width_loc, axis=0)]
    later = [(p * tp_count + t) for p in range(1, section_count) for t in range(tp_count)]
    for shift in range(1, tp_count):
        outgoing_rows = lax.dynamic_slice_in_dim(
            weight_own, ((my_tp + shift) % tp_count) * width_loc, width_loc, axis=0
        )
        route = [(i, i - i % tp_count + (i % tp_count + shift) % tp_count) for i in later]
        relative_rows.append(lax.ppermute(outgoing_rows, ("pipe", "tp"), route))
    weight_rows = jnp.concatenate(relative_rows, axis=1)
    block_order = (my_tp - jnp.arange(tp_count, dtype=jnp.int32)) % tp_count
    carried = jnp.zeros((rows_per, width_loc), jnp.bfloat16)
    section_rows = jnp.zeros((RQ * S, width_loc), jnp.bfloat16)
    fresh_rows = jnp.zeros((RQ * S, 2, kv_width), jnp.bfloat16)
    for tick_id in range(batches + section_count - 1):
        offset_batch = tick_id - section_id
        active = (offset_batch >= 0) & (offset_batch < batches)
        if tick_id == 0:
            hstate = hidden
            whole_rows = lax.all_gather(hstate, "tp", axis=1, tiled=True)
            widened = whole_rows.astype(jnp.float32)
            inv_rms = lax.rsqrt(jnp.mean(widened * widened, axis=-1, keepdims=True) + 1e-05)
            normed = (widened * inv_rms * gain_full).astype(jnp.bfloat16)
            projected = jnp.dot(normed, weight_flat, preferred_element_type=jnp.float32)
        else:
            hstate = carried
            widened = hstate.astype(jnp.float32)
            scaled = (widened * gain_own).astype(jnp.bfloat16)
            part_rel = jnp.dot(scaled, weight_rows, preferred_element_type=jnp.float32).reshape(
                rows_per, tp_count, 2 * kv_width
            )
            part_abs = jnp.swapaxes(jnp.take(part_rel, block_order, axis=1), 0, 1)
            sumsq = jnp.sum(widened * widened, axis=-1)
            sumsq_rows = jnp.zeros((tp_count, 8, 2 * kv_width), jnp.float32).at[:, 0, :rows_per].set(
                jnp.broadcast_to(sumsq, (tp_count, rows_per))
            )
            got = exchange(
                jnp.concatenate([part_abs, sumsq_rows], axis=1), "tp", 10 + tick_id, gate=tick_id
            )
            got = jnp.sum(got, axis=0)
            inv_rms = lax.rsqrt(got[rows_per, :rows_per] / D + 1e-05)
            projected = got[:rows_per] * inv_rms[:, None]
        projected = projected.reshape(rows_per, 2, kv_heads, HD)
        new_keys = rotate(projected[:, 0], positions).astype(jnp.bfloat16)
        new_values = projected[:, 1].astype(jnp.bfloat16)
        fresh_kv = jnp.stack(
            [new_keys.reshape(rows_per, kv_width), new_values.reshape(rows_per, kv_width)], axis=1
        )
        gathered = layer_pages[page_table]
        cached = jnp.swapaxes(gathered, 1, 2).reshape(per_batch, 2, CTX, kv_heads, HD)
        fresh_heads = fresh_kv.reshape(per_batch, S, 2, kv_heads, HD)
        query_heads = queries[0].reshape(per_batch, S, kv_heads, group_size, HD)
        score_old = jnp.einsum(
            "bskgd,btkd->bskgt", query_heads, cached[:, 0], preferred_element_type=jnp.float32
        ) * HD ** (-0.5)
        score_new = jnp.einsum(
            "bskgd,btkd->bskgt",
            query_heads,
            fresh_heads[:, :, 0],
            preferred_element_type=jnp.float32,
        ) * HD ** (-0.5)
        old_ok = key_pos[None, :] < lengths[:, None]
        score_old = jnp.where(old_ok[:, None, None, None, :], score_old, -jnp.inf)
        score_new = jnp.where(causal[None, :, None, None, :], score_new, -jnp.inf)
        row_max = jnp.maximum(jnp.max(score_old, axis=-1), jnp.max(score_new, axis=-1))[..., None]
        exp_old = jnp.exp(score_old - row_max)
        exp_new = jnp.exp(score_new - row_max)
        denominator = (jnp.sum(exp_old, axis=-1) + jnp.sum(exp_new, axis=-1))[..., None]
        weight_old = (exp_old / denominator).astype(jnp.bfloat16)
        weight_new = (exp_new / denominator).astype(jnp.bfloat16)
        mixed = jnp.einsum(
            "bskgt,btkd->bskgd", weight_old, cached[:, 1], preferred_element_type=jnp.float32
        )
        mixed = mixed + jnp.einsum(
            "bskgt,btkd->bskgd",
            weight_new,
            fresh_heads[:, :, 1],
            preferred_element_type=jnp.float32,
        )
        attended = mixed.reshape(per_batch, S, q_width).astype(jnp.bfloat16)
        outgoing = (
            jnp.zeros((req_count, batch_cap, S, q_width), jnp.bfloat16)
            .at[dest_all, slot_all]
            .set(attended)
        )
        rows_in = exchange(outgoing, "req", 20 + tick_id, gate=tick_id)
        sources = rows_in.shape[0]
        item_count = rows_in.shape[1]
        flat_rows = rows_in.reshape(sources * item_count * S, q_width)
        all_low = jnp.einsum(
            "nf,arf->nar", flat_rows, adapters_in, preferred_element_type=jnp.float32
        )
        picks_rows = jnp.broadcast_to(picks_in[:, :, None], (sources, item_count, S)).reshape(
            sources * item_count * S
        )
        one_hot = (picks_rows[:, None] == adapter_slots[None, :]).astype(jnp.float32)
        partial_low = jnp.sum(all_low * one_hot[:, :, None], axis=1)
        rank_low = jnp.sum(exchange(partial_low, "tp", 30 + tick_id, gather=True, gate=tick_id), axis=0).astype(jnp.bfloat16)
        spread = (rank_low.astype(jnp.float32)[:, None, :] * one_hot[:, :, None]).astype(
            jnp.bfloat16
        )
        deltas = jnp.dot(
            spread.reshape(sources * item_count * S, ADP_DEV * R),
            adapters_out,
            preferred_element_type=jnp.float32,
        ).astype(jnp.bfloat16)
        deltas = deltas.reshape(sources, item_count, S, width_loc)
        returned = exchange(deltas, "req", 40 + tick_id, gate=tick_id)
        delta_rows = returned[dest_all, slot_all].reshape(rows_per, width_loc)
        new_state = (hstate.astype(jnp.float32) + delta_rows.astype(jnp.float32)).astype(
            jnp.bfloat16
        )
        section_rows = jnp.where(active, new_state, section_rows)
        fresh_rows = jnp.where(active, fresh_kv, fresh_rows)
        if tick_id + 1 < section_count:
            carried = passed_along(new_state, "pipe", tick_id)
        sent_pages = lax.cond(section_id == tick_id, build_pages, no_pages, fresh_kv)
        got_pages = exchange(sent_pages, "req", 50 + tick_id, gate=tick_id)
        landed = jnp.dot(
            land_pick, got_pages.reshape(box_count, -1), preferred_element_type=jnp.float32
        ).astype(jnp.bfloat16)
        arrived = jnp.where(
            section_id == tick_id, landed.reshape(free_slots, 2, PAGE, kv_width), arrived
        )

    return (section_rows[None], fresh_rows[None], arrived[None])


def solution(mesh):
    in_specs = (
        P("req", "tp"),
        P("pipe", "req", "tp"),
        P("pipe", None),
        P("pipe", None, None, "tp"),
        P("pipe", "req", None, "tp"),
        P("pipe", "req", None, "tp"),
        P("pipe", "req", None, None, "tp"),
        P("req"),
        P(),
        P("req", None),
        P("req"),
        P("req", None),
    )
    out_specs = (
        P("pipe", "req", "tp"),
        P("pipe", "req", None, "tp"),
        P("pipe", "req", None, None, "tp"),
    )
    return jax.shard_map(body, mesh=mesh, in_specs=in_specs, out_specs=out_specs, check_vma=False)
```

```python
import functools
import math

import jax
import jax.numpy as jnp
from jax import lax
from jax.experimental import pallas as pl
from jax.experimental.pallas import tpu as pltpu
from jax.sharding import PartitionSpec as P

D = 8192
HD = 128
R = 64
ADP_DEV = 4
RQ = 32
S = 4
MICRO = 2
PAGE = 64
MOVES = 16
RQ_MB = 16
CTX = 256


def passed_along(block, axis, source):
    return lax.ppermute(block, axis, [(source, source + 1)])


def exchange_kernel(axis, n, gather, gate, x_ref, o_ref, send_sem, recv_sem, local_sem):
    if gate is None:
        exchange_body(axis, n, gather, x_ref, o_ref, send_sem, recv_sem, local_sem)
    else:
        pl.when(lax.axis_index("pipe") == gate)(
            lambda: exchange_body(axis, n, gather, x_ref, o_ref, send_sem, recv_sem, local_sem)
        )


def exchange_body(axis, n, gather, x_ref, o_ref, send_sem, recv_sem, local_sem):
    me = lax.axis_index(axis)
    barrier = pltpu.get_barrier_semaphore()
    for j in range(1, n):
        pl.semaphore_signal(
            barrier, 1, device_id={axis: (me + j) % n}, device_id_type=pl.DeviceIdType.MESH
        )
    pl.semaphore_wait(barrier, n - 1)
    copies = []
    for j in range(1, n):
        peer = (me + j) % n
        copy = pltpu.make_async_remote_copy(
            src_ref=x_ref if gather else x_ref.at[peer],
            dst_ref=o_ref.at[me],
            send_sem=send_sem.at[j],
            recv_sem=recv_sem.at[j],
            device_id={axis: peer},
            device_id_type=pl.DeviceIdType.MESH,
        )
        copy.start()
        copies.append(copy)
    local = pltpu.make_async_copy(x_ref if gather else x_ref.at[me], o_ref.at[me], local_sem)
    local.start()
    local.wait()
    for copy in copies:
        copy.wait()


def exchange(x, axis, collective_id, gather=False, gate=None):
    n = lax.axis_size(axis)
    out_shape = (n,) + x.shape if gather else x.shape
    return pl.pallas_call(
        functools.partial(exchange_kernel, axis, n, gather, gate),
        out_shape=jax.ShapeDtypeStruct(out_shape, x.dtype),
        in_specs=[pl.BlockSpec(memory_space=pl.ANY)],
        out_specs=pl.BlockSpec(memory_space=pl.ANY),
        scratch_shapes=[
            pltpu.SemaphoreType.DMA((n,)),
            pltpu.SemaphoreType.DMA((n,)),
            pltpu.SemaphoreType.DMA(()),
        ],
        compiler_params=pltpu.CompilerParams(collective_id=collective_id, has_side_effects=True),
    )(x)


def rotate(key_vecs, positions):
    half_dim = key_vecs.shape[-1] // 2
    inv_freq = jnp.exp(
        -math.log(500000.0) * (2.0 * jnp.arange(half_dim, dtype=jnp.float32) / key_vecs.shape[-1])
    )
    angles = positions.astype(jnp.float32)[..., None, None] * inv_freq
    cos_vals = jnp.cos(angles)
    sin_vals = jnp.sin(angles)
    front_half = key_vecs[..., :half_dim]
    back_half = key_vecs[..., half_dim:]
    return jnp.concatenate(
        [
            front_half * cos_vals - back_half * sin_vals,
            back_half * cos_vals + front_half * sin_vals,
        ],
        axis=-1,
    )


def body(
    hidden,
    queries,
    norm_gain,
    kv_weight,
    adapter_in,
    adapter_out,
    kv_pages,
    adapter_ids,
    owner_rows,
    page_table,
    lengths,
    moves,
):
    section_count = lax.axis_size("pipe")
    req_count = lax.axis_size("req")
    section_id = lax.axis_index("pipe")
    my_req = lax.axis_index("req")
    width_loc = hidden.shape[1]
    q_width = queries.shape[2]
    kv_width = kv_weight.shape[3]
    kv_heads = kv_width // HD
    group_size = q_width // HD // kv_heads
    batches = 1
    per_batch = RQ // batches
    rows_per = per_batch * S
    block_cap = min(RQ_MB, max(2, 2 * RQ_MB // req_count))
    batch_cap = block_cap * (MICRO // batches)
    pair_cap = (MOVES + req_count - 2) // (req_count - 1)
    free_slots = (req_count - 1) * pair_cap
    token_ids = jnp.arange(S, dtype=jnp.int32)
    store_rows = owner_rows[adapter_ids]
    dest_all = store_rows // ADP_DEV
    pick_all = store_rows % ADP_DEV
    req_ids = jnp.arange(RQ, dtype=jnp.int32)
    earlier = (
        (req_ids[None, :] < req_ids[:, None])
        & (req_ids[None, :] // per_batch == req_ids[:, None] // per_batch)
        & (dest_all[None, :] == dest_all[:, None])
    )
    slot_all = jnp.sum(earlier.astype(jnp.int32), axis=1)
    positions = (lengths[:, None] + token_ids[None, :]).reshape(RQ * S)
    gain_full = norm_gain[0].astype(jnp.float32)
    weight_flat = kv_weight[0].reshape(D, 2 * kv_width)
    layer_pages = kv_pages[0]
    adapters_in = adapter_in[0]
    adapters_out = adapter_out[0].reshape(ADP_DEV * R, width_loc)
    key_pos = jnp.arange(CTX, dtype=jnp.int32)
    causal = token_ids[None, :] <= token_ids[:, None]
    adapter_slots = jnp.arange(ADP_DEV, dtype=jnp.int32)
    move_ids = jnp.arange(MOVES, dtype=jnp.int32)
    move_dest = moves[:, 0]
    move_slot = jnp.sum(
        (
            (move_ids[None, :] < move_ids[:, None]) & (move_dest[None, :] == move_dest[:, None])
        ).astype(jnp.int32),
        axis=1,
    )
    picks_out = jnp.zeros((req_count, batch_cap), jnp.int32).at[dest_all, slot_all].set(pick_all)
    spots_out = jnp.full((req_count, pair_cap), -1, jnp.int32).at[move_dest, move_slot].set(moves[:, 2])
    ints_in = lax.all_to_all(
        jnp.concatenate([picks_out, spots_out], axis=1), "req", split_axis=0, concat_axis=0, tiled=True
    )
    picks_in = ints_in[:, :batch_cap]
    spots_in = ints_in[:, batch_cap:].reshape(req_count * pair_cap)
    spot_match = spots_in[None, :] == jnp.arange(free_slots, dtype=jnp.int32)[:, None]
    has_page = jnp.any(spot_match, axis=1)
    page_src = jnp.argmax(spot_match, axis=1)
    box_ids = jnp.arange(req_count * pair_cap, dtype=jnp.int32)
    box_match = (move_dest * pair_cap + move_slot)[None, :] == box_ids[:, None]
    box_move = jnp.argmax(box_match, axis=1)
    box_used = jnp.any(box_match, axis=1)
    box_page = jnp.where(box_used, moves[box_move, 1], -1)
    box_pick = (box_page[:, None] == jnp.arange(layer_pages.shape[0], dtype=jnp.int32)[None, :]).astype(
        jnp.bfloat16
    )
    land_pick = (spot_match & has_page[:, None]).astype(jnp.bfloat16)
    box_count = req_count * pair_cap

    def build_base():
        return jnp.dot(
            box_pick, layer_pages.reshape(layer_pages.shape[0], -1), preferred_element_type=jnp.float32
        ).astype(jnp.bfloat16).reshape(box_count, 2, PAGE, kv_width)

    def no_base():
        return jnp.zeros((box_count, 2, PAGE, kv_width), jnp.bfloat16)

    base_early = lax.cond(section_id != 0, build_base, no_base)

    def build_pages(fresh):
        spot_ids = jnp.arange(req_count * pair_cap * PAGE, dtype=jnp.int32)
        tok_match = tok_spot[None, :] == spot_ids[:, None]
        tok_pick = tok_match.astype(jnp.bfloat16)
        tok_hit = jnp.any(tok_match, axis=1).reshape(req_count * pair_cap, PAGE)
        base = lax.cond(section_id == 0, build_base, lambda: base_early)
        patch = jnp.dot(
            tok_pick, fresh.reshape(RQ * S, 2 * kv_width), preferred_element_type=jnp.float32
        ).astype(jnp.bfloat16)
        patch = jnp.swapaxes(patch.reshape(box_count, PAGE, 2, kv_width), 1, 2)
        return jnp.where(tok_hit[:, None, :, None], patch, base).reshape(
            req_count, pair_cap, 2, PAGE, kv_width
        )

    def no_pages(fresh):
        return jnp.zeros((req_count, pair_cap, 2, PAGE, kv_width), jnp.bfloat16)

    arrived = jnp.zeros((free_slots, 2, PAGE, kv_width), jnp.bfloat16)
    page_slot = jnp.take_along_axis(page_table, (positions // PAGE).reshape(RQ, S), axis=1).reshape(
        RQ * S
    )
    tok_in_box = page_slot[:, None] == box_page[None, :]
    tok_spot = jnp.where(
        jnp.any(tok_in_box, axis=1),
        jnp.argmax(tok_in_box, axis=1).astype(jnp.int32) * PAGE + positions % PAGE,
        -1,
    )
    tp_count = lax.axis_size("tp")
    my_tp = lax.axis_index("tp")
    gain_own = lax.dynamic_slice_in_dim(gain_full, my_tp * width_loc, width_loc)
    weight_own = kv_weight[0].reshape(D, 2 * kv_width)
    relative_rows = [lax.dynamic_slice_in_dim(weight_own, my_tp * width_loc, width_loc, axis=0)]
    later = [(p * tp_count + t) for p in range(1, section_count) for t in range(tp_count)]
    for shift in range(1, tp_count):
        outgoing_rows = lax.dynamic_slice_in_dim(
            weight_own, ((my_tp + shift) % tp_count) * width_loc, width_loc, axis=0
        )
        route = [(i, i - i % tp_count + (i % tp_count + shift) % tp_count) for i in later]
        relative_rows.append(lax.ppermute(outgoing_rows, ("pipe", "tp"), route))
    weight_rows = jnp.concatenate(relative_rows, axis=1)
    block_order = (my_tp - jnp.arange(tp_count, dtype=jnp.int32)) % tp_count
    carried = jnp.zeros((rows_per, width_loc), jnp.bfloat16)
    section_rows = jnp.zeros((RQ * S, width_loc), jnp.bfloat16)
    fresh_rows = jnp.zeros((RQ * S, 2, kv_width), jnp.bfloat16)
    for tick_id in range(batches + section_count - 1):
        offset_batch = tick_id - section_id
        active = (offset_batch >= 0) & (offset_batch < batches)
        if tick_id == 0:
            hstate = hidden
            whole_rows = lax.all_gather(hstate, "tp", axis=1, tiled=True)
            widened = whole_rows.astype(jnp.float32)
            inv_rms = lax.rsqrt(jnp.mean(widened * widened, axis=-1, keepdims=True) + 1e-05)
            normed = (widened * inv_rms * gain_full).astype(jnp.bfloat16)
            projected = jnp.dot(normed, weight_flat, preferred_element_type=jnp.float32)
        else:
            hstate = carried
            widened = hstate.astype(jnp.float32)
            scaled = (widened * gain_own).astype(jnp.bfloat16)
            part_rel = jnp.dot(scaled, weight_rows, preferred_element_type=jnp.float32).reshape(
                rows_per, tp_count, 2 * kv_width
            )
            part_abs = jnp.swapaxes(jnp.take(part_rel, block_order, axis=1), 0, 1)
            sumsq = jnp.sum(widened * widened, axis=-1)
            sumsq_rows = jnp.zeros((tp_count, 8, 2 * kv_width), jnp.float32).at[:, 0, :rows_per].set(
                jnp.broadcast_to(sumsq, (tp_count, rows_per))
            )
            got = exchange(
                jnp.concatenate([part_abs, sumsq_rows], axis=1), "tp", 10 + tick_id, gate=tick_id
            )
            got = jnp.sum(got, axis=0)
            inv_rms = lax.rsqrt(got[rows_per, :rows_per] / D + 1e-05)
            projected = got[:rows_per] * inv_rms[:, None]
        projected = projected.reshape(rows_per, 2, kv_heads, HD)
        new_keys = rotate(projected[:, 0], positions).astype(jnp.bfloat16)
        new_values = projected[:, 1].astype(jnp.bfloat16)
        fresh_kv = jnp.stack(
            [new_keys.reshape(rows_per, kv_width), new_values.reshape(rows_per, kv_width)], axis=1
        )
        gathered = layer_pages[page_table]
        cached = jnp.swapaxes(gathered, 1, 2).reshape(per_batch, 2, CTX, kv_heads, HD)
        fresh_heads = fresh_kv.reshape(per_batch, S, 2, kv_heads, HD)
        query_heads = queries[0].reshape(per_batch, S, kv_heads, group_size, HD)
        score_old = jnp.einsum(
            "bskgd,btkd->bskgt", query_heads, cached[:, 0], preferred_element_type=jnp.float32
        ) * HD ** (-0.5)
        score_new = jnp.einsum(
            "bskgd,btkd->bskgt",
            query_heads,
            fresh_heads[:, :, 0],
            preferred_element_type=jnp.float32,
        ) * HD ** (-0.5)
        old_ok = key_pos[None, :] < lengths[:, None]
        score_old = jnp.where(old_ok[:, None, None, None, :], score_old, -jnp.inf)
        score_new = jnp.where(causal[None, :, None, None, :], score_new, -jnp.inf)
        row_max = jnp.maximum(jnp.max(score_old, axis=-1), jnp.max(score_new, axis=-1))[..., None]
        exp_old = jnp.exp(score_old - row_max)
        exp_new = jnp.exp(score_new - row_max)
        denominator = (jnp.sum(exp_old, axis=-1) + jnp.sum(exp_new, axis=-1))[..., None]
        weight_old = (exp_old / denominator).astype(jnp.bfloat16)
        weight_new = (exp_new / denominator).astype(jnp.bfloat16)
        mixed = jnp.einsum(
            "bskgt,btkd->bskgd", weight_old, cached[:, 1], preferred_element_type=jnp.float32
        )
        mixed = mixed + jnp.einsum(
            "bskgt,btkd->bskgd",
            weight_new,
            fresh_heads[:, :, 1],
            preferred_element_type=jnp.float32,
        )
        attended = mixed.reshape(per_batch, S, q_width).astype(jnp.bfloat16)
        outgoing = (
            jnp.zeros((req_count, batch_cap, S, q_width), jnp.bfloat16)
            .at[dest_all, slot_all]
            .set(attended)
        )
        rows_in = exchange(outgoing, "req", 20 + tick_id, gate=tick_id)
        sources = rows_in.shape[0]
        item_count = rows_in.shape[1]
        flat_rows = rows_in.reshape(sources * item_count * S, q_width)
        all_low = jnp.einsum(
            "nf,arf->nar", flat_rows, adapters_in, preferred_element_type=jnp.float32
        )
        picks_rows = jnp.broadcast_to(picks_in[:, :, None], (sources, item_count, S)).reshape(
            sources * item_count * S
        )
        one_hot = (picks_rows[:, None] == adapter_slots[None, :]).astype(jnp.float32)
        partial_low = jnp.sum(all_low * one_hot[:, :, None], axis=1)
        rank_low = jnp.sum(exchange(partial_low, "tp", 30 + tick_id, gather=True, gate=tick_id), axis=0).astype(jnp.bfloat16)
        spread = (rank_low.astype(jnp.float32)[:, None, :] * one_hot[:, :, None]).astype(
            jnp.bfloat16
        )
        deltas = jnp.dot(
            spread.reshape(sources * item_count * S, ADP_DEV * R),
            adapters_out,
            preferred_element_type=jnp.float32,
        ).astype(jnp.bfloat16)
        deltas = deltas.reshape(sources, item_count, S, width_loc)
        returned = exchange(deltas, "req", 40 + tick_id, gate=tick_id)
        delta_rows = returned[dest_all, slot_all].reshape(rows_per, width_loc)
        new_state = (hstate.astype(jnp.float32) + delta_rows.astype(jnp.float32)).astype(
            jnp.bfloat16
        )
        section_rows = jnp.where(active, new_state, section_rows)
        fresh_rows = jnp.where(active, fresh_kv, fresh_rows)
        if tick_id + 1 < section_count:
            carried = passed_along(new_state, "pipe", tick_id)
        sent_pages = lax.cond(section_id == tick_id, build_pages, no_pages, fresh_kv)
        got_pages = exchange(sent_pages, "req", 50 + tick_id, gate=tick_id)
        landed = jnp.dot(
            land_pick, got_pages.reshape(box_count, -1), preferred_element_type=jnp.float32
        ).astype(jnp.bfloat16)
        arrived = jnp.where(
            section_id == tick_id, landed.reshape(free_slots, 2, PAGE, kv_width), arrived
        )

    return (section_rows[None], fresh_rows[None], arrived[None])


def solution(mesh):
    in_specs = (
        P("req", "tp"),
        P("pipe", "req", "tp"),
        P("pipe", None),
        P("pipe", None, None, "tp"),
        P("pipe", "req", None, "tp"),
        P("pipe", "req", None, "tp"),
        P("pipe", "req", None, None, "tp"),
        P("req"),
        P(),
        P("req", None),
        P("req"),
        P("req", None),
    )
    out_specs = (
        P("pipe", "req", "tp"),
        P("pipe", "req", None, "tp"),
        P("pipe", "req", None, None, "tp"),
    )
    return jax.shard_map(body, mesh=mesh, in_specs=in_specs, out_specs=out_specs, check_vma=False)
```

```python
import functools
import math

import jax
import jax.numpy as jnp
from jax import lax
from jax.experimental import pallas as pl
from jax.experimental.pallas import tpu as pltpu
from jax.sharding import PartitionSpec as P

D = 8192
HD = 128
R = 64
ADP_DEV = 4
RQ = 32
S = 4
MICRO = 2
PAGE = 64
MOVES = 16
RQ_MB = 16
CTX = 256


def passed_along(block, axis, source):
    return lax.ppermute(block, axis, [(source, source + 1)])


def exchange_kernel(axis, n, gather, gate, x_ref, o_ref, send_sem, recv_sem, local_sem):
    if gate is None:
        exchange_body(axis, n, gather, x_ref, o_ref, send_sem, recv_sem, local_sem)
    else:
        pl.when(lax.axis_index("pipe") == gate)(
            lambda: exchange_body(axis, n, gather, x_ref, o_ref, send_sem, recv_sem, local_sem)
        )


def exchange_body(axis, n, gather, x_ref, o_ref, send_sem, recv_sem, local_sem):
    me = lax.axis_index(axis)
    barrier = pltpu.get_barrier_semaphore()
    for j in range(1, n):
        pl.semaphore_signal(
            barrier, 1, device_id={axis: (me + j) % n}, device_id_type=pl.DeviceIdType.MESH
        )
    pl.semaphore_wait(barrier, n - 1)
    copies = []
    for j in range(1, n):
        peer = (me + j) % n
        copy = pltpu.make_async_remote_copy(
            src_ref=x_ref if gather else x_ref.at[peer],
            dst_ref=o_ref.at[me],
            send_sem=send_sem.at[j],
            recv_sem=recv_sem.at[j],
            device_id={axis: peer},
            device_id_type=pl.DeviceIdType.MESH,
        )
        copy.start()
        copies.append(copy)
    local = pltpu.make_async_copy(x_ref if gather else x_ref.at[me], o_ref.at[me], local_sem)
    local.start()
    local.wait()
    for copy in copies:
        copy.wait()


def exchange(x, axis, collective_id, gather=False, gate=None):
    n = lax.axis_size(axis)
    out_shape = (n,) + x.shape if gather else x.shape
    return pl.pallas_call(
        functools.partial(exchange_kernel, axis, n, gather, gate),
        out_shape=jax.ShapeDtypeStruct(out_shape, x.dtype),
        in_specs=[pl.BlockSpec(memory_space=pl.ANY)],
        out_specs=pl.BlockSpec(memory_space=pl.ANY),
        scratch_shapes=[
            pltpu.SemaphoreType.DMA((n,)),
            pltpu.SemaphoreType.DMA((n,)),
            pltpu.SemaphoreType.DMA(()),
        ],
        compiler_params=pltpu.CompilerParams(collective_id=collective_id, has_side_effects=True),
    )(x)


def rotate(key_vecs, positions):
    half_dim = key_vecs.shape[-1] // 2
    inv_freq = jnp.exp(
        -math.log(500000.0) * (2.0 * jnp.arange(half_dim, dtype=jnp.float32) / key_vecs.shape[-1])
    )
    angles = positions.astype(jnp.float32)[..., None, None] * inv_freq
    cos_vals = jnp.cos(angles)
    sin_vals = jnp.sin(angles)
    front_half = key_vecs[..., :half_dim]
    back_half = key_vecs[..., half_dim:]
    return jnp.concatenate(
        [
            front_half * cos_vals - back_half * sin_vals,
            back_half * cos_vals + front_half * sin_vals,
        ],
        axis=-1,
    )


def body(
    hidden,
    queries,
    norm_gain,
    kv_weight,
    adapter_in,
    adapter_out,
    kv_pages,
    adapter_ids,
    owner_rows,
    page_table,
    lengths,
    moves,
):
    section_count = lax.axis_size("pipe")
    req_count = lax.axis_size("req")
    section_id = lax.axis_index("pipe")
    my_req = lax.axis_index("req")
    width_loc = hidden.shape[1]
    q_width = queries.shape[2]
    kv_width = kv_weight.shape[3]
    kv_heads = kv_width // HD
    group_size = q_width // HD // kv_heads
    batches = 1
    per_batch = RQ // batches
    rows_per = per_batch * S
    block_cap = min(RQ_MB, max(2, 2 * RQ_MB // req_count))
    batch_cap = block_cap * (MICRO // batches)
    pair_cap = (MOVES + req_count - 2) // (req_count - 1)
    free_slots = (req_count - 1) * pair_cap
    token_ids = jnp.arange(S, dtype=jnp.int32)
    store_rows = owner_rows[adapter_ids]
    dest_all = store_rows // ADP_DEV
    pick_all = store_rows % ADP_DEV
    req_ids = jnp.arange(RQ, dtype=jnp.int32)
    earlier = (
        (req_ids[None, :] < req_ids[:, None])
        & (req_ids[None, :] // per_batch == req_ids[:, None] // per_batch)
        & (dest_all[None, :] == dest_all[:, None])
    )
    slot_all = jnp.sum(earlier.astype(jnp.int32), axis=1)
    positions = (lengths[:, None] + token_ids[None, :]).reshape(RQ * S)
    gain_full = norm_gain[0].astype(jnp.float32)
    weight_flat = kv_weight[0].reshape(D, 2 * kv_width)
    layer_pages = kv_pages[0]
    adapters_in = adapter_in[0]
    adapters_out = adapter_out[0].reshape(ADP_DEV * R, width_loc)
    key_pos = jnp.arange(CTX, dtype=jnp.int32)
    causal = token_ids[None, :] <= token_ids[:, None]
    adapter_slots = jnp.arange(ADP_DEV, dtype=jnp.int32)
    move_ids = jnp.arange(MOVES, dtype=jnp.int32)
    move_dest = moves[:, 0]
    move_slot = jnp.sum(
        (
            (move_ids[None, :] < move_ids[:, None]) & (move_dest[None, :] == move_dest[:, None])
        ).astype(jnp.int32),
        axis=1,
    )
    picks_out = jnp.zeros((req_count, batch_cap), jnp.int32).at[dest_all, slot_all].set(pick_all)
    spots_out = jnp.full((req_count, pair_cap), -1, jnp.int32).at[move_dest, move_slot].set(moves[:, 2])
    ints_in = lax.all_to_all(
        jnp.concatenate([picks_out, spots_out], axis=1), "req", split_axis=0, concat_axis=0, tiled=True
    )
    picks_in = ints_in[:, :batch_cap]
    spots_in = ints_in[:, batch_cap:].reshape(req_count * pair_cap)
    spot_match = spots_in[None, :] == jnp.arange(free_slots, dtype=jnp.int32)[:, None]
    has_page = jnp.any(spot_match, axis=1)
    page_src = jnp.argmax(spot_match, axis=1)
    box_ids = jnp.arange(req_count * pair_cap, dtype=jnp.int32)
    box_match = (move_dest * pair_cap + move_slot)[None, :] == box_ids[:, None]
    box_move = jnp.argmax(box_match, axis=1)
    box_used = jnp.any(box_match, axis=1)
    box_page = jnp.where(box_used, moves[box_move, 1], -1)
    box_pick = (box_page[:, None] == jnp.arange(layer_pages.shape[0], dtype=jnp.int32)[None, :]).astype(
        jnp.bfloat16
    )
    land_pick = (spot_match & has_page[:, None]).astype(jnp.bfloat16)
    box_count = req_count * pair_cap

    def build_pages(fresh):
        spot_ids = jnp.arange(req_count * pair_cap * PAGE, dtype=jnp.int32)
        tok_match = tok_spot[None, :] == spot_ids[:, None]
        tok_pick = tok_match.astype(jnp.bfloat16)
        tok_hit = jnp.any(tok_match, axis=1).reshape(req_count * pair_cap, PAGE)
        base = jnp.dot(
            box_pick, layer_pages.reshape(layer_pages.shape[0], -1), preferred_element_type=jnp.float32
        ).astype(jnp.bfloat16).reshape(box_count, 2, PAGE, kv_width)
        patch = jnp.dot(
            tok_pick, fresh.reshape(RQ * S, 2 * kv_width), preferred_element_type=jnp.float32
        ).astype(jnp.bfloat16)
        patch = jnp.swapaxes(patch.reshape(box_count, PAGE, 2, kv_width), 1, 2)
        return jnp.where(tok_hit[:, None, :, None], patch, base).reshape(
            req_count, pair_cap, 2, PAGE, kv_width
        )

    def no_pages(fresh):
        return jnp.zeros((req_count, pair_cap, 2, PAGE, kv_width), jnp.bfloat16)

    arrived = jnp.zeros((free_slots, 2, PAGE, kv_width), jnp.bfloat16)
    page_slot = jnp.take_along_axis(page_table, (positions // PAGE).reshape(RQ, S), axis=1).reshape(
        RQ * S
    )
    tok_in_box = page_slot[:, None] == box_page[None, :]
    tok_spot = jnp.where(
        jnp.any(tok_in_box, axis=1),
        jnp.argmax(tok_in_box, axis=1).astype(jnp.int32) * PAGE + positions % PAGE,
        -1,
    )
    tp_count = lax.axis_size("tp")
    my_tp = lax.axis_index("tp")
    gain_own = lax.dynamic_slice_in_dim(gain_full, my_tp * width_loc, width_loc)
    weight_own = kv_weight[0].reshape(D, 2 * kv_width)

    def shuffle_rows(weight_src):
        relative_rows = [lax.dynamic_slice_in_dim(weight_src, my_tp * width_loc, width_loc, axis=0)]
        later = [(p * tp_count + t) for p in range(1, section_count) for t in range(tp_count)]
        for shift in range(1, tp_count):
            outgoing_rows = lax.dynamic_slice_in_dim(
                weight_src, ((my_tp + shift) % tp_count) * width_loc, width_loc, axis=0
            )
            route = [(i, i - i % tp_count + (i % tp_count + shift) % tp_count) for i in later]
            relative_rows.append(lax.ppermute(outgoing_rows, ("pipe", "tp"), route))
        return jnp.concatenate(relative_rows, axis=1)
    block_order = (my_tp - jnp.arange(tp_count, dtype=jnp.int32)) % tp_count
    carried = jnp.zeros((rows_per, width_loc), jnp.bfloat16)
    section_rows = jnp.zeros((RQ * S, width_loc), jnp.bfloat16)
    fresh_rows = jnp.zeros((RQ * S, 2, kv_width), jnp.bfloat16)
    for tick_id in range(batches + section_count - 1):
        offset_batch = tick_id - section_id
        active = (offset_batch >= 0) & (offset_batch < batches)
        if tick_id == 0:
            hstate = hidden
            whole_rows = lax.all_gather(hstate, "tp", axis=1, tiled=True)
            widened = whole_rows.astype(jnp.float32)
            inv_rms = lax.rsqrt(jnp.mean(widened * widened, axis=-1, keepdims=True) + 1e-05)
            normed = (widened * inv_rms * gain_full).astype(jnp.bfloat16)
            projected = jnp.dot(normed, weight_flat, preferred_element_type=jnp.float32)
        else:
            hstate = carried
            widened = hstate.astype(jnp.float32)
            scaled = (widened * gain_own).astype(jnp.bfloat16)
            part_rel = jnp.dot(scaled, weight_rows, preferred_element_type=jnp.float32).reshape(
                rows_per, tp_count, 2 * kv_width
            )
            part_abs = jnp.swapaxes(jnp.take(part_rel, block_order, axis=1), 0, 1)
            sumsq = jnp.sum(widened * widened, axis=-1)
            sumsq_rows = jnp.zeros((tp_count, 8, 2 * kv_width), jnp.float32).at[:, 0, :rows_per].set(
                jnp.broadcast_to(sumsq, (tp_count, rows_per))
            )
            got = exchange(
                jnp.concatenate([part_abs, sumsq_rows], axis=1), "tp", 10 + tick_id, gate=tick_id
            )
            got = jnp.sum(got, axis=0)
            inv_rms = lax.rsqrt(got[rows_per, :rows_per] / D + 1e-05)
            projected = got[:rows_per] * inv_rms[:, None]
        projected = projected.reshape(rows_per, 2, kv_heads, HD)
        new_keys = rotate(projected[:, 0], positions).astype(jnp.bfloat16)
        new_values = projected[:, 1].astype(jnp.bfloat16)
        fresh_kv = jnp.stack(
            [new_keys.reshape(rows_per, kv_width), new_values.reshape(rows_per, kv_width)], axis=1
        )
        gathered = layer_pages[page_table]
        cached = jnp.swapaxes(gathered, 1, 2).reshape(per_batch, 2, CTX, kv_heads, HD)
        fresh_heads = fresh_kv.reshape(per_batch, S, 2, kv_heads, HD)
        query_heads = queries[0].reshape(per_batch, S, kv_heads, group_size, HD)
        score_old = jnp.einsum(
            "bskgd,btkd->bskgt", query_heads, cached[:, 0], preferred_element_type=jnp.float32
        ) * HD ** (-0.5)
        score_new = jnp.einsum(
            "bskgd,btkd->bskgt",
            query_heads,
            fresh_heads[:, :, 0],
            preferred_element_type=jnp.float32,
        ) * HD ** (-0.5)
        old_ok = key_pos[None, :] < lengths[:, None]
        score_old = jnp.where(old_ok[:, None, None, None, :], score_old, -jnp.inf)
        score_new = jnp.where(causal[None, :, None, None, :], score_new, -jnp.inf)
        row_max = jnp.maximum(jnp.max(score_old, axis=-1), jnp.max(score_new, axis=-1))[..., None]
        exp_old = jnp.exp(score_old - row_max)
        exp_new = jnp.exp(score_new - row_max)
        denominator = (jnp.sum(exp_old, axis=-1) + jnp.sum(exp_new, axis=-1))[..., None]
        weight_old = (exp_old / denominator).astype(jnp.bfloat16)
        weight_new = (exp_new / denominator).astype(jnp.bfloat16)
        mixed = jnp.einsum(
            "bskgt,btkd->bskgd", weight_old, cached[:, 1], preferred_element_type=jnp.float32
        )
        mixed = mixed + jnp.einsum(
            "bskgt,btkd->bskgd",
            weight_new,
            fresh_heads[:, :, 1],
            preferred_element_type=jnp.float32,
        )
        attended = mixed.reshape(per_batch, S, q_width).astype(jnp.bfloat16)
        outgoing = (
            jnp.zeros((req_count, batch_cap, S, q_width), jnp.bfloat16)
            .at[dest_all, slot_all]
            .set(attended)
        )
        rows_in = exchange(outgoing, "req", 20 + tick_id, gate=tick_id)
        sources = rows_in.shape[0]
        item_count = rows_in.shape[1]
        flat_rows = rows_in.reshape(sources * item_count * S, q_width)
        all_low = jnp.einsum(
            "nf,arf->nar", flat_rows, adapters_in, preferred_element_type=jnp.float32
        )
        picks_rows = jnp.broadcast_to(picks_in[:, :, None], (sources, item_count, S)).reshape(
            sources * item_count * S
        )
        one_hot = (picks_rows[:, None] == adapter_slots[None, :]).astype(jnp.float32)
        partial_low = jnp.sum(all_low * one_hot[:, :, None], axis=1)
        rank_low = jnp.sum(exchange(partial_low, "tp", 30 + tick_id, gather=True, gate=tick_id), axis=0).astype(jnp.bfloat16)
        spread = (rank_low.astype(jnp.float32)[:, None, :] * one_hot[:, :, None]).astype(
            jnp.bfloat16
        )
        deltas = jnp.dot(
            spread.reshape(sources * item_count * S, ADP_DEV * R),
            adapters_out,
            preferred_element_type=jnp.float32,
        ).astype(jnp.bfloat16)
        deltas = deltas.reshape(sources, item_count, S, width_loc)
        returned = exchange(deltas, "req", 40 + tick_id, gate=tick_id)
        delta_rows = returned[dest_all, slot_all].reshape(rows_per, width_loc)
        new_state = (hstate.astype(jnp.float32) + delta_rows.astype(jnp.float32)).astype(
            jnp.bfloat16
        )
        section_rows = jnp.where(active, new_state, section_rows)
        fresh_rows = jnp.where(active, fresh_kv, fresh_rows)
        if tick_id + 1 < section_count:
            carried = passed_along(new_state, "pipe", tick_id)
        if tick_id == 0:
            weight_src, _ = lax.optimization_barrier((weight_own, new_state))
            weight_rows = shuffle_rows(weight_src)
        sent_pages = lax.cond(section_id == tick_id, build_pages, no_pages, fresh_kv)
        got_pages = exchange(sent_pages, "req", 50 + tick_id, gate=tick_id)
        landed = jnp.dot(
            land_pick, got_pages.reshape(box_count, -1), preferred_element_type=jnp.float32
        ).astype(jnp.bfloat16)
        arrived = jnp.where(
            section_id == tick_id, landed.reshape(free_slots, 2, PAGE, kv_width), arrived
        )

    return (section_rows[None], fresh_rows[None], arrived[None])


def solution(mesh):
    in_specs = (
        P("req", "tp"),
        P("pipe", "req", "tp"),
        P("pipe", None),
        P("pipe", None, None, "tp"),
        P("pipe", "req", None, "tp"),
        P("pipe", "req", None, "tp"),
        P("pipe", "req", None, None, "tp"),
        P("req"),
        P(),
        P("req", None),
        P("req"),
        P("req", None),
    )
    out_specs = (
        P("pipe", "req", "tp"),
        P("pipe", "req", None, "tp"),
        P("pipe", "req", None, None, "tp"),
    )
    return jax.shard_map(body, mesh=mesh, in_specs=in_specs, out_specs=out_specs, check_vma=False)
```

```python
import functools
import math

import jax
import jax.numpy as jnp
from jax import lax
from jax.experimental import pallas as pl
from jax.experimental.pallas import tpu as pltpu
from jax.sharding import PartitionSpec as P

D = 8192
HD = 128
R = 64
ADP_DEV = 4
RQ = 32
S = 4
MICRO = 2
PAGE = 64
MOVES = 16
RQ_MB = 16
CTX = 256


def passed_along(block, axis, source):
    return lax.ppermute(block, axis, [(source, source + 1)])


def exchange_kernel(axis, n, gather, gate, x_ref, o_ref, send_sem, recv_sem, local_sem):
    if gate is None:
        exchange_body(axis, n, gather, x_ref, o_ref, send_sem, recv_sem, local_sem)
    else:
        pl.when(lax.axis_index("pipe") == gate)(
            lambda: exchange_body(axis, n, gather, x_ref, o_ref, send_sem, recv_sem, local_sem)
        )


def exchange_body(axis, n, gather, x_ref, o_ref, send_sem, recv_sem, local_sem):
    me = lax.axis_index(axis)
    barrier = pltpu.get_barrier_semaphore()
    for j in range(1, n):
        pl.semaphore_signal(
            barrier, 1, device_id={axis: (me + j) % n}, device_id_type=pl.DeviceIdType.MESH
        )
    pl.semaphore_wait(barrier, n - 1)
    copies = []
    for j in range(1, n):
        peer = (me + j) % n
        copy = pltpu.make_async_remote_copy(
            src_ref=x_ref if gather else x_ref.at[peer],
            dst_ref=o_ref.at[me],
            send_sem=send_sem.at[j],
            recv_sem=recv_sem.at[j],
            device_id={axis: peer},
            device_id_type=pl.DeviceIdType.MESH,
        )
        copy.start()
        copies.append(copy)
    local = pltpu.make_async_copy(x_ref if gather else x_ref.at[me], o_ref.at[me], local_sem)
    local.start()
    local.wait()
    for copy in copies:
        copy.wait()


def exchange(x, axis, collective_id, gather=False, gate=None):
    n = lax.axis_size(axis)
    out_shape = (n,) + x.shape if gather else x.shape
    return pl.pallas_call(
        functools.partial(exchange_kernel, axis, n, gather, gate),
        out_shape=jax.ShapeDtypeStruct(out_shape, x.dtype),
        in_specs=[pl.BlockSpec(memory_space=pl.ANY)],
        out_specs=pl.BlockSpec(memory_space=pl.ANY),
        scratch_shapes=[
            pltpu.SemaphoreType.DMA((n,)),
            pltpu.SemaphoreType.DMA((n,)),
            pltpu.SemaphoreType.DMA(()),
        ],
        compiler_params=pltpu.CompilerParams(collective_id=collective_id, has_side_effects=True),
    )(x)


def rotate(key_vecs, positions):
    half_dim = key_vecs.shape[-1] // 2
    inv_freq = jnp.exp(
        -math.log(500000.0) * (2.0 * jnp.arange(half_dim, dtype=jnp.float32) / key_vecs.shape[-1])
    )
    angles = positions.astype(jnp.float32)[..., None, None] * inv_freq
    cos_vals = jnp.cos(angles)
    sin_vals = jnp.sin(angles)
    front_half = key_vecs[..., :half_dim]
    back_half = key_vecs[..., half_dim:]
    return jnp.concatenate(
        [
            front_half * cos_vals - back_half * sin_vals,
            back_half * cos_vals + front_half * sin_vals,
        ],
        axis=-1,
    )


def body(
    hidden,
    queries,
    norm_gain,
    kv_weight,
    adapter_in,
    adapter_out,
    kv_pages,
    adapter_ids,
    owner_rows,
    page_table,
    lengths,
    moves,
):
    section_count = lax.axis_size("pipe")
    req_count = lax.axis_size("req")
    section_id = lax.axis_index("pipe")
    my_req = lax.axis_index("req")
    width_loc = hidden.shape[1]
    q_width = queries.shape[2]
    kv_width = kv_weight.shape[3]
    kv_heads = kv_width // HD
    group_size = q_width // HD // kv_heads
    batches = 1
    per_batch = RQ // batches
    rows_per = per_batch * S
    block_cap = min(RQ_MB, max(2, 2 * RQ_MB // req_count))
    batch_cap = block_cap * (MICRO // batches)
    pair_cap = (MOVES + req_count - 2) // (req_count - 1)
    free_slots = (req_count - 1) * pair_cap
    token_ids = jnp.arange(S, dtype=jnp.int32)
    store_rows = owner_rows[adapter_ids]
    dest_all = store_rows // ADP_DEV
    pick_all = store_rows % ADP_DEV
    req_ids = jnp.arange(RQ, dtype=jnp.int32)
    earlier = (
        (req_ids[None, :] < req_ids[:, None])
        & (req_ids[None, :] // per_batch == req_ids[:, None] // per_batch)
        & (dest_all[None, :] == dest_all[:, None])
    )
    slot_all = jnp.sum(earlier.astype(jnp.int32), axis=1)
    positions = (lengths[:, None] + token_ids[None, :]).reshape(RQ * S)
    gain_full = norm_gain[0].astype(jnp.float32)
    weight_flat = kv_weight[0].reshape(D, 2 * kv_width)
    layer_pages = kv_pages[0]
    adapters_in = adapter_in[0]
    adapters_out = adapter_out[0].reshape(ADP_DEV * R, width_loc)
    key_pos = jnp.arange(CTX, dtype=jnp.int32)
    causal = token_ids[None, :] <= token_ids[:, None]
    adapter_slots = jnp.arange(ADP_DEV, dtype=jnp.int32)
    move_ids = jnp.arange(MOVES, dtype=jnp.int32)
    move_dest = moves[:, 0]
    move_slot = jnp.sum(
        (
            (move_ids[None, :] < move_ids[:, None]) & (move_dest[None, :] == move_dest[:, None])
        ).astype(jnp.int32),
        axis=1,
    )
    picks_out = jnp.zeros((req_count, batch_cap), jnp.int32).at[dest_all, slot_all].set(pick_all)
    spots_out = jnp.full((req_count, pair_cap), -1, jnp.int32).at[move_dest, move_slot].set(moves[:, 2])
    ints_in = lax.all_to_all(
        jnp.concatenate([picks_out, spots_out], axis=1), "req", split_axis=0, concat_axis=0, tiled=True
    )
    picks_in = ints_in[:, :batch_cap]
    spots_in = ints_in[:, batch_cap:].reshape(req_count * pair_cap)
    spot_match = spots_in[None, :] == jnp.arange(free_slots, dtype=jnp.int32)[:, None]
    has_page = jnp.any(spot_match, axis=1)
    page_src = jnp.argmax(spot_match, axis=1)
    box_ids = jnp.arange(req_count * pair_cap, dtype=jnp.int32)
    box_match = (move_dest * pair_cap + move_slot)[None, :] == box_ids[:, None]
    box_move = jnp.argmax(box_match, axis=1)
    box_used = jnp.any(box_match, axis=1)
    box_page = jnp.where(box_used, moves[box_move, 1], -1)
    box_pick = (box_page[:, None] == jnp.arange(layer_pages.shape[0], dtype=jnp.int32)[None, :]).astype(
        jnp.bfloat16
    )
    land_pick = (spot_match & has_page[:, None]).astype(jnp.bfloat16)
    box_count = req_count * pair_cap

    def build_base():
        return jnp.dot(
            box_pick, layer_pages.reshape(layer_pages.shape[0], -1), preferred_element_type=jnp.float32
        ).astype(jnp.bfloat16).reshape(box_count, 2, PAGE, kv_width)

    def no_base():
        return jnp.zeros((box_count, 2, PAGE, kv_width), jnp.bfloat16)

    base_early = lax.cond(section_id != 0, build_base, no_base)

    def build_pages(fresh):
        spot_ids = jnp.arange(req_count * pair_cap * PAGE, dtype=jnp.int32)
        tok_match = tok_spot[None, :] == spot_ids[:, None]
        tok_pick = tok_match.astype(jnp.bfloat16)
        tok_hit = jnp.any(tok_match, axis=1).reshape(req_count * pair_cap, PAGE)
        base = lax.cond(section_id == 0, build_base, lambda: base_early)
        patch = jnp.dot(
            tok_pick, fresh.reshape(RQ * S, 2 * kv_width), preferred_element_type=jnp.float32
        ).astype(jnp.bfloat16)
        patch = jnp.swapaxes(patch.reshape(box_count, PAGE, 2, kv_width), 1, 2)
        return jnp.where(tok_hit[:, None, :, None], patch, base).reshape(
            req_count, pair_cap, 2, PAGE, kv_width
        )

    def no_pages(fresh):
        return jnp.zeros((req_count, pair_cap, 2, PAGE, kv_width), jnp.bfloat16)

    arrived = jnp.zeros((free_slots, 2, PAGE, kv_width), jnp.bfloat16)
    page_slot = jnp.take_along_axis(page_table, (positions // PAGE).reshape(RQ, S), axis=1).reshape(
        RQ * S
    )
    tok_in_box = page_slot[:, None] == box_page[None, :]
    tok_spot = jnp.where(
        jnp.any(tok_in_box, axis=1),
        jnp.argmax(tok_in_box, axis=1).astype(jnp.int32) * PAGE + positions % PAGE,
        -1,
    )
    tp_count = lax.axis_size("tp")
    my_tp = lax.axis_index("tp")
    gain_own = lax.dynamic_slice_in_dim(gain_full, my_tp * width_loc, width_loc)
    weight_own = kv_weight[0].reshape(D, 2 * kv_width)

    def shuffle_rows(weight_src):
        relative_rows = [lax.dynamic_slice_in_dim(weight_src, my_tp * width_loc, width_loc, axis=0)]
        later = [(p * tp_count + t) for p in range(1, section_count) for t in range(tp_count)]
        for shift in range(1, tp_count):
            outgoing_rows = lax.dynamic_slice_in_dim(
                weight_src, ((my_tp + shift) % tp_count) * width_loc, width_loc, axis=0
            )
            route = [(i, i - i % tp_count + (i % tp_count + shift) % tp_count) for i in later]
            relative_rows.append(lax.ppermute(outgoing_rows, ("pipe", "tp"), route))
        return jnp.concatenate(relative_rows, axis=1)
    block_order = (my_tp - jnp.arange(tp_count, dtype=jnp.int32)) % tp_count
    carried = jnp.zeros((rows_per, width_loc), jnp.bfloat16)
    section_rows = jnp.zeros((RQ * S, width_loc), jnp.bfloat16)
    fresh_rows = jnp.zeros((RQ * S, 2, kv_width), jnp.bfloat16)
    for tick_id in range(batches + section_count - 1):
        offset_batch = tick_id - section_id
        active = (offset_batch >= 0) & (offset_batch < batches)
        if tick_id == 0:
            hstate = hidden
            whole_rows = lax.all_gather(hstate, "tp", axis=1, tiled=True)
            widened = whole_rows.astype(jnp.float32)
            inv_rms = lax.rsqrt(jnp.mean(widened * widened, axis=-1, keepdims=True) + 1e-05)
            normed = (widened * inv_rms * gain_full).astype(jnp.bfloat16)
            projected = jnp.dot(normed, weight_flat, preferred_element_type=jnp.float32)
        else:
            hstate = carried
            widened = hstate.astype(jnp.float32)
            scaled = (widened * gain_own).astype(jnp.bfloat16)
            part_rel = jnp.dot(scaled, weight_rows, preferred_element_type=jnp.float32).reshape(
                rows_per, tp_count, 2 * kv_width
            )
            part_abs = jnp.swapaxes(jnp.take(part_rel, block_order, axis=1), 0, 1)
            sumsq = jnp.sum(widened * widened, axis=-1)
            sumsq_rows = jnp.zeros((tp_count, 8, 2 * kv_width), jnp.float32).at[:, 0, :rows_per].set(
                jnp.broadcast_to(sumsq, (tp_count, rows_per))
            )
            got = exchange(
                jnp.concatenate([part_abs, sumsq_rows], axis=1), "tp", 10 + tick_id, gate=tick_id
            )
            got = jnp.sum(got, axis=0)
            inv_rms = lax.rsqrt(got[rows_per, :rows_per] / D + 1e-05)
            projected = got[:rows_per] * inv_rms[:, None]
        projected = projected.reshape(rows_per, 2, kv_heads, HD)
        new_keys = rotate(projected[:, 0], positions).astype(jnp.bfloat16)
        new_values = projected[:, 1].astype(jnp.bfloat16)
        fresh_kv = jnp.stack(
            [new_keys.reshape(rows_per, kv_width), new_values.reshape(rows_per, kv_width)], axis=1
        )
        gathered = layer_pages[page_table]
        cached = jnp.swapaxes(gathered, 1, 2).reshape(per_batch, 2, CTX, kv_heads, HD)
        fresh_heads = fresh_kv.reshape(per_batch, S, 2, kv_heads, HD)
        query_heads = queries[0].reshape(per_batch, S, kv_heads, group_size, HD)
        score_old = jnp.einsum(
            "bskgd,btkd->bskgt", query_heads, cached[:, 0], preferred_element_type=jnp.float32
        ) * HD ** (-0.5)
        score_new = jnp.einsum(
            "bskgd,btkd->bskgt",
            query_heads,
            fresh_heads[:, :, 0],
            preferred_element_type=jnp.float32,
        ) * HD ** (-0.5)
        old_ok = key_pos[None, :] < lengths[:, None]
        score_old = jnp.where(old_ok[:, None, None, None, :], score_old, -jnp.inf)
        score_new = jnp.where(causal[None, :, None, None, :], score_new, -jnp.inf)
        row_max = jnp.maximum(jnp.max(score_old, axis=-1), jnp.max(score_new, axis=-1))[..., None]
        exp_old = jnp.exp(score_old - row_max)
        exp_new = jnp.exp(score_new - row_max)
        denominator = (jnp.sum(exp_old, axis=-1) + jnp.sum(exp_new, axis=-1))[..., None]
        weight_old = (exp_old / denominator).astype(jnp.bfloat16)
        weight_new = (exp_new / denominator).astype(jnp.bfloat16)
        mixed = jnp.einsum(
            "bskgt,btkd->bskgd", weight_old, cached[:, 1], preferred_element_type=jnp.float32
        )
        mixed = mixed + jnp.einsum(
            "bskgt,btkd->bskgd",
            weight_new,
            fresh_heads[:, :, 1],
            preferred_element_type=jnp.float32,
        )
        attended = mixed.reshape(per_batch, S, q_width).astype(jnp.bfloat16)
        outgoing = (
            jnp.zeros((req_count, batch_cap, S, q_width), jnp.bfloat16)
            .at[dest_all, slot_all]
            .set(attended)
        )
        rows_in = exchange(outgoing, "req", 20 + tick_id, gate=tick_id)
        sources = rows_in.shape[0]
        item_count = rows_in.shape[1]
        flat_rows = rows_in.reshape(sources * item_count * S, q_width)
        all_low = jnp.einsum(
            "nf,arf->nar", flat_rows, adapters_in, preferred_element_type=jnp.float32
        )
        picks_rows = jnp.broadcast_to(picks_in[:, :, None], (sources, item_count, S)).reshape(
            sources * item_count * S
        )
        one_hot = (picks_rows[:, None] == adapter_slots[None, :]).astype(jnp.float32)
        partial_low = jnp.sum(all_low * one_hot[:, :, None], axis=1)
        rank_low = jnp.sum(exchange(partial_low, "tp", 30 + tick_id, gather=True, gate=tick_id), axis=0).astype(jnp.bfloat16)
        spread = (rank_low.astype(jnp.float32)[:, None, :] * one_hot[:, :, None]).astype(
            jnp.bfloat16
        )
        deltas = jnp.dot(
            spread.reshape(sources * item_count * S, ADP_DEV * R),
            adapters_out,
            preferred_element_type=jnp.float32,
        ).astype(jnp.bfloat16)
        deltas = deltas.reshape(sources, item_count, S, width_loc)
        returned = exchange(deltas, "req", 40 + tick_id, gate=tick_id)
        delta_rows = returned[dest_all, slot_all].reshape(rows_per, width_loc)
        new_state = (hstate.astype(jnp.float32) + delta_rows.astype(jnp.float32)).astype(
            jnp.bfloat16
        )
        section_rows = jnp.where(active, new_state, section_rows)
        fresh_rows = jnp.where(active, fresh_kv, fresh_rows)
        if tick_id + 1 < section_count:
            carried = passed_along(new_state, "pipe", tick_id)
        if tick_id == 0:
            weight_src, _ = lax.optimization_barrier((weight_own, new_state))
            weight_rows = shuffle_rows(weight_src)
        sent_pages = lax.cond(section_id == tick_id, build_pages, no_pages, fresh_kv)
        got_pages = exchange(sent_pages, "req", 50 + tick_id, gate=tick_id)
        landed = jnp.dot(
            land_pick, got_pages.reshape(box_count, -1), preferred_element_type=jnp.float32
        ).astype(jnp.bfloat16)
        arrived = jnp.where(
            section_id == tick_id, landed.reshape(free_slots, 2, PAGE, kv_width), arrived
        )

    return (section_rows[None], fresh_rows[None], arrived[None])


def solution(mesh):
    in_specs = (
        P("req", "tp"),
        P("pipe", "req", "tp"),
        P("pipe", None),
        P("pipe", None, None, "tp"),
        P("pipe", "req", None, "tp"),
        P("pipe", "req", None, "tp"),
        P("pipe", "req", None, None, "tp"),
        P("req"),
        P(),
        P("req", None),
        P("req"),
        P("req", None),
    )
    out_specs = (
        P("pipe", "req", "tp"),
        P("pipe", "req", None, "tp"),
        P("pipe", "req", None, None, "tp"),
    )
    return jax.shard_map(body, mesh=mesh, in_specs=in_specs, out_specs=out_specs, check_vma=False)
```

```python
import functools
import math

import jax
import jax.numpy as jnp
from jax import lax
from jax.experimental import pallas as pl
from jax.experimental.pallas import tpu as pltpu
from jax.sharding import PartitionSpec as P

D = 8192
HD = 128
R = 64
ADP_DEV = 4
RQ = 32
S = 4
MICRO = 2
PAGE = 64
MOVES = 16
RQ_MB = 16
CTX = 256


def passed_along(block, axis, source):
    return lax.ppermute(block, axis, [(source, source + 1)])


def exchange_kernel(axis, n, gather, gate, x_ref, o_ref, send_sem, recv_sem, local_sem):
    if gate is None:
        exchange_body(axis, n, gather, x_ref, o_ref, send_sem, recv_sem, local_sem)
    else:
        pl.when(lax.axis_index("pipe") == gate)(
            lambda: exchange_body(axis, n, gather, x_ref, o_ref, send_sem, recv_sem, local_sem)
        )


def exchange_body(axis, n, gather, x_ref, o_ref, send_sem, recv_sem, local_sem):
    me = lax.axis_index(axis)
    barrier = pltpu.get_barrier_semaphore()
    for j in range(1, n):
        pl.semaphore_signal(
            barrier, 1, device_id={axis: (me + j) % n}, device_id_type=pl.DeviceIdType.MESH
        )
    pl.semaphore_wait(barrier, n - 1)
    copies = []
    for j in range(1, n):
        peer = (me + j) % n
        copy = pltpu.make_async_remote_copy(
            src_ref=x_ref if gather else x_ref.at[peer],
            dst_ref=o_ref.at[me],
            send_sem=send_sem.at[j],
            recv_sem=recv_sem.at[j],
            device_id={axis: peer},
            device_id_type=pl.DeviceIdType.MESH,
        )
        copy.start()
        copies.append(copy)
    local = pltpu.make_async_copy(x_ref if gather else x_ref.at[me], o_ref.at[me], local_sem)
    local.start()
    local.wait()
    for copy in copies:
        copy.wait()


def exchange(x, axis, collective_id, gather=False, gate=None):
    n = lax.axis_size(axis)
    out_shape = (n,) + x.shape if gather else x.shape
    return pl.pallas_call(
        functools.partial(exchange_kernel, axis, n, gather, gate),
        out_shape=jax.ShapeDtypeStruct(out_shape, x.dtype),
        in_specs=[pl.BlockSpec(memory_space=pl.ANY)],
        out_specs=pl.BlockSpec(memory_space=pl.ANY),
        scratch_shapes=[
            pltpu.SemaphoreType.DMA((n,)),
            pltpu.SemaphoreType.DMA((n,)),
            pltpu.SemaphoreType.DMA(()),
        ],
        compiler_params=pltpu.CompilerParams(collective_id=collective_id, has_side_effects=True),
    )(x)


def rotate(key_vecs, positions):
    half_dim = key_vecs.shape[-1] // 2
    inv_freq = jnp.exp(
        -math.log(500000.0) * (2.0 * jnp.arange(half_dim, dtype=jnp.float32) / key_vecs.shape[-1])
    )
    angles = positions.astype(jnp.float32)[..., None, None] * inv_freq
    cos_vals = jnp.cos(angles)
    sin_vals = jnp.sin(angles)
    front_half = key_vecs[..., :half_dim]
    back_half = key_vecs[..., half_dim:]
    return jnp.concatenate(
        [
            front_half * cos_vals - back_half * sin_vals,
            back_half * cos_vals + front_half * sin_vals,
        ],
        axis=-1,
    )


def body(
    hidden,
    queries,
    norm_gain,
    kv_weight,
    adapter_in,
    adapter_out,
    kv_pages,
    adapter_ids,
    owner_rows,
    page_table,
    lengths,
    moves,
):
    section_count = lax.axis_size("pipe")
    req_count = lax.axis_size("req")
    section_id = lax.axis_index("pipe")
    my_req = lax.axis_index("req")
    width_loc = hidden.shape[1]
    q_width = queries.shape[2]
    kv_width = kv_weight.shape[3]
    kv_heads = kv_width // HD
    group_size = q_width // HD // kv_heads
    batches = 1
    per_batch = RQ // batches
    rows_per = per_batch * S
    block_cap = min(RQ_MB, max(2, 2 * RQ_MB // req_count))
    batch_cap = block_cap * (MICRO // batches)
    pair_cap = (MOVES + req_count - 2) // (req_count - 1)
    free_slots = (req_count - 1) * pair_cap
    token_ids = jnp.arange(S, dtype=jnp.int32)
    store_rows = owner_rows[adapter_ids]
    dest_all = store_rows // ADP_DEV
    pick_all = store_rows % ADP_DEV
    req_ids = jnp.arange(RQ, dtype=jnp.int32)
    earlier = (
        (req_ids[None, :] < req_ids[:, None])
        & (req_ids[None, :] // per_batch == req_ids[:, None] // per_batch)
        & (dest_all[None, :] == dest_all[:, None])
    )
    slot_all = jnp.sum(earlier.astype(jnp.int32), axis=1)
    positions = (lengths[:, None] + token_ids[None, :]).reshape(RQ * S)
    gain_full = norm_gain[0].astype(jnp.float32)
    weight_flat = kv_weight[0].reshape(D, 2 * kv_width)
    layer_pages = kv_pages[0]
    adapters_in = adapter_in[0]
    adapters_out = adapter_out[0].reshape(ADP_DEV * R, width_loc)
    key_pos = jnp.arange(CTX, dtype=jnp.int32)
    causal = token_ids[None, :] <= token_ids[:, None]
    adapter_slots = jnp.arange(ADP_DEV, dtype=jnp.int32)
    move_ids = jnp.arange(MOVES, dtype=jnp.int32)
    move_dest = moves[:, 0]
    move_slot = jnp.sum(
        (
            (move_ids[None, :] < move_ids[:, None]) & (move_dest[None, :] == move_dest[:, None])
        ).astype(jnp.int32),
        axis=1,
    )
    picks_out = jnp.zeros((req_count, batch_cap), jnp.int32).at[dest_all, slot_all].set(pick_all)
    spots_out = jnp.full((req_count, pair_cap), -1, jnp.int32).at[move_dest, move_slot].set(moves[:, 2])
    ints_in = lax.all_to_all(
        jnp.concatenate([picks_out, spots_out], axis=1), "req", split_axis=0, concat_axis=0, tiled=True
    )
    picks_in = ints_in[:, :batch_cap]
    spots_in = ints_in[:, batch_cap:].reshape(req_count * pair_cap)
    spot_match = spots_in[None, :] == jnp.arange(free_slots, dtype=jnp.int32)[:, None]
    has_page = jnp.any(spot_match, axis=1)
    page_src = jnp.argmax(spot_match, axis=1)
    box_ids = jnp.arange(req_count * pair_cap, dtype=jnp.int32)
    box_match = (move_dest * pair_cap + move_slot)[None, :] == box_ids[:, None]
    box_move = jnp.argmax(box_match, axis=1)
    box_used = jnp.any(box_match, axis=1)
    box_page = jnp.where(box_used, moves[box_move, 1], -1)
    box_pick = (box_page[:, None] == jnp.arange(layer_pages.shape[0], dtype=jnp.int32)[None, :]).astype(
        jnp.bfloat16
    )
    land_pick = (spot_match & has_page[:, None]).astype(jnp.bfloat16)
    box_count = req_count * pair_cap

    def build_pages(fresh):
        spot_ids = jnp.arange(req_count * pair_cap * PAGE, dtype=jnp.int32)
        tok_match = tok_spot[None, :] == spot_ids[:, None]
        tok_pick = tok_match.astype(jnp.bfloat16)
        tok_hit = jnp.any(tok_match, axis=1).reshape(req_count * pair_cap, PAGE)
        base = jnp.einsum(
            "bp,pcjk->bcjk", box_pick, layer_pages, preferred_element_type=jnp.float32
        ).astype(jnp.bfloat16)
        patch = jnp.dot(
            tok_pick, fresh.reshape(RQ * S, 2 * kv_width), preferred_element_type=jnp.float32
        ).astype(jnp.bfloat16)
        patch = jnp.swapaxes(patch.reshape(box_count, PAGE, 2, kv_width), 1, 2)
        return jnp.where(tok_hit[:, None, :, None], patch, base).reshape(
            req_count, pair_cap, 2, PAGE, kv_width
        )

    def no_pages(fresh):
        return jnp.zeros((req_count, pair_cap, 2, PAGE, kv_width), jnp.bfloat16)

    arrived = jnp.zeros((free_slots, 2, PAGE, kv_width), jnp.bfloat16)
    page_slot = jnp.take_along_axis(page_table, (positions // PAGE).reshape(RQ, S), axis=1).reshape(
        RQ * S
    )
    tok_in_box = page_slot[:, None] == box_page[None, :]
    tok_spot = jnp.where(
        jnp.any(tok_in_box, axis=1),
        jnp.argmax(tok_in_box, axis=1).astype(jnp.int32) * PAGE + positions % PAGE,
        -1,
    )
    tp_count = lax.axis_size("tp")
    my_tp = lax.axis_index("tp")
    gain_own = lax.dynamic_slice_in_dim(gain_full, my_tp * width_loc, width_loc)
    weight_own = kv_weight[0].reshape(D, 2 * kv_width)

    def shuffle_rows(weight_src):
        relative_rows = [lax.dynamic_slice_in_dim(weight_src, my_tp * width_loc, width_loc, axis=0)]
        later = [(p * tp_count + t) for p in range(1, section_count) for t in range(tp_count)]
        for shift in range(1, tp_count):
            outgoing_rows = lax.dynamic_slice_in_dim(
                weight_src, ((my_tp + shift) % tp_count) * width_loc, width_loc, axis=0
            )
            route = [(i, i - i % tp_count + (i % tp_count + shift) % tp_count) for i in later]
            relative_rows.append(lax.ppermute(outgoing_rows, ("pipe", "tp"), route))
        return jnp.concatenate(relative_rows, axis=1)
    block_order = (my_tp - jnp.arange(tp_count, dtype=jnp.int32)) % tp_count
    carried = jnp.zeros((rows_per, width_loc), jnp.bfloat16)
    section_rows = jnp.zeros((RQ * S, width_loc), jnp.bfloat16)
    fresh_rows = jnp.zeros((RQ * S, 2, kv_width), jnp.bfloat16)
    for tick_id in range(batches + section_count - 1):
        offset_batch = tick_id - section_id
        active = (offset_batch >= 0) & (offset_batch < batches)
        if tick_id == 0:
            hstate = hidden
            whole_rows = lax.all_gather(hstate, "tp", axis=1, tiled=True)
            widened = whole_rows.astype(jnp.float32)
            inv_rms = lax.rsqrt(jnp.mean(widened * widened, axis=-1, keepdims=True) + 1e-05)
            normed = (widened * inv_rms * gain_full).astype(jnp.bfloat16)
            projected = jnp.dot(normed, weight_flat, preferred_element_type=jnp.float32)
        else:
            hstate = carried
            widened = hstate.astype(jnp.float32)
            scaled = (widened * gain_own).astype(jnp.bfloat16)
            part_rel = jnp.dot(scaled, weight_rows, preferred_element_type=jnp.float32).reshape(
                rows_per, tp_count, 2 * kv_width
            )
            part_abs = jnp.swapaxes(jnp.take(part_rel, block_order, axis=1), 0, 1)
            sumsq = jnp.sum(widened * widened, axis=-1)
            sumsq_rows = jnp.zeros((tp_count, 8, 2 * kv_width), jnp.float32).at[:, 0, :rows_per].set(
                jnp.broadcast_to(sumsq, (tp_count, rows_per))
            )
            got = exchange(
                jnp.concatenate([part_abs, sumsq_rows], axis=1), "tp", 10 + tick_id, gate=tick_id
            )
            got = jnp.sum(got, axis=0)
            inv_rms = lax.rsqrt(got[rows_per, :rows_per] / D + 1e-05)
            projected = got[:rows_per] * inv_rms[:, None]
        projected = projected.reshape(rows_per, 2, kv_heads, HD)
        new_keys = rotate(projected[:, 0], positions).astype(jnp.bfloat16)
        new_values = projected[:, 1].astype(jnp.bfloat16)
        fresh_kv = jnp.stack(
            [new_keys.reshape(rows_per, kv_width), new_values.reshape(rows_per, kv_width)], axis=1
        )
        gathered = layer_pages[page_table]
        cached = jnp.swapaxes(gathered, 1, 2).reshape(per_batch, 2, CTX, kv_heads, HD)
        fresh_heads = fresh_kv.reshape(per_batch, S, 2, kv_heads, HD)
        query_heads = queries[0].reshape(per_batch, S, kv_heads, group_size, HD)
        score_old = jnp.einsum(
            "bskgd,btkd->bskgt", query_heads, cached[:, 0], preferred_element_type=jnp.float32
        ) * HD ** (-0.5)
        score_new = jnp.einsum(
            "bskgd,btkd->bskgt",
            query_heads,
            fresh_heads[:, :, 0],
            preferred_element_type=jnp.float32,
        ) * HD ** (-0.5)
        old_ok = key_pos[None, :] < lengths[:, None]
        score_old = jnp.where(old_ok[:, None, None, None, :], score_old, -jnp.inf)
        score_new = jnp.where(causal[None, :, None, None, :], score_new, -jnp.inf)
        row_max = jnp.maximum(jnp.max(score_old, axis=-1), jnp.max(score_new, axis=-1))[..., None]
        exp_old = jnp.exp(score_old - row_max)
        exp_new = jnp.exp(score_new - row_max)
        denominator = (jnp.sum(exp_old, axis=-1) + jnp.sum(exp_new, axis=-1))[..., None]
        weight_old = (exp_old / denominator).astype(jnp.bfloat16)
        weight_new = (exp_new / denominator).astype(jnp.bfloat16)
        mixed = jnp.einsum(
            "bskgt,btkd->bskgd", weight_old, cached[:, 1], preferred_element_type=jnp.float32
        )
        mixed = mixed + jnp.einsum(
            "bskgt,btkd->bskgd",
            weight_new,
            fresh_heads[:, :, 1],
            preferred_element_type=jnp.float32,
        )
        attended = mixed.reshape(per_batch, S, q_width).astype(jnp.bfloat16)
        outgoing = (
            jnp.zeros((req_count, batch_cap, S, q_width), jnp.bfloat16)
            .at[dest_all, slot_all]
            .set(attended)
        )
        rows_in = exchange(outgoing, "req", 20 + tick_id, gate=tick_id)
        sources = rows_in.shape[0]
        item_count = rows_in.shape[1]
        flat_rows = rows_in.reshape(sources * item_count * S, q_width)
        all_low = jnp.einsum(
            "nf,arf->nar", flat_rows, adapters_in, preferred_element_type=jnp.float32
        )
        picks_rows = jnp.broadcast_to(picks_in[:, :, None], (sources, item_count, S)).reshape(
            sources * item_count * S
        )
        one_hot = (picks_rows[:, None] == adapter_slots[None, :]).astype(jnp.float32)
        partial_low = jnp.sum(all_low * one_hot[:, :, None], axis=1)
        rank_low = jnp.sum(exchange(partial_low, "tp", 30 + tick_id, gather=True, gate=tick_id), axis=0).astype(jnp.bfloat16)
        spread = (rank_low.astype(jnp.float32)[:, None, :] * one_hot[:, :, None]).astype(
            jnp.bfloat16
        )
        deltas = jnp.dot(
            spread.reshape(sources * item_count * S, ADP_DEV * R),
            adapters_out,
            preferred_element_type=jnp.float32,
        ).astype(jnp.bfloat16)
        deltas = deltas.reshape(sources, item_count, S, width_loc)
        returned = exchange(deltas, "req", 40 + tick_id, gate=tick_id)
        delta_rows = returned[dest_all, slot_all].reshape(rows_per, width_loc)
        new_state = (hstate.astype(jnp.float32) + delta_rows.astype(jnp.float32)).astype(
            jnp.bfloat16
        )
        section_rows = jnp.where(active, new_state, section_rows)
        fresh_rows = jnp.where(active, fresh_kv, fresh_rows)
        if tick_id + 1 < section_count:
            carried = passed_along(new_state, "pipe", tick_id)
        if tick_id == 0:
            weight_src, _ = lax.optimization_barrier((weight_own, new_state))
            weight_rows = shuffle_rows(weight_src)
        sent_pages = lax.cond(section_id == tick_id, build_pages, no_pages, fresh_kv)
        got_pages = exchange(sent_pages, "req", 50 + tick_id, gate=tick_id)
        landed = jnp.einsum(
            "fb,bcjk->fcjk",
            land_pick,
            got_pages.reshape(box_count, 2, PAGE, kv_width),
            preferred_element_type=jnp.float32,
        ).astype(jnp.bfloat16)
        arrived = jnp.where(section_id == tick_id, landed, arrived)

    return (section_rows[None], fresh_rows[None], arrived[None])


def solution(mesh):
    in_specs = (
        P("req", "tp"),
        P("pipe", "req", "tp"),
        P("pipe", None),
        P("pipe", None, None, "tp"),
        P("pipe", "req", None, "tp"),
        P("pipe", "req", None, "tp"),
        P("pipe", "req", None, None, "tp"),
        P("req"),
        P(),
        P("req", None),
        P("req"),
        P("req", None),
    )
    out_specs = (
        P("pipe", "req", "tp"),
        P("pipe", "req", None, "tp"),
        P("pipe", "req", None, None, "tp"),
    )
    return jax.shard_map(body, mesh=mesh, in_specs=in_specs, out_specs=out_specs, check_vma=False)
```

```python
import functools
import math

import jax
import jax.numpy as jnp
from jax import lax
from jax.experimental import pallas as pl
from jax.experimental.pallas import tpu as pltpu
from jax.sharding import PartitionSpec as P

D = 8192
HD = 128
R = 64
ADP_DEV = 4
RQ = 32
S = 4
MICRO = 2
PAGE = 64
MOVES = 16
RQ_MB = 16
CTX = 256


def passed_along(block, axis, source):
    return lax.ppermute(block, axis, [(source, source + 1)])


def exchange_kernel(axis, n, gather, gate, x_ref, o_ref, send_sem, recv_sem, local_sem):
    if gate is None:
        exchange_body(axis, n, gather, x_ref, o_ref, send_sem, recv_sem, local_sem)
    else:
        pl.when(lax.axis_index("pipe") == gate)(
            lambda: exchange_body(axis, n, gather, x_ref, o_ref, send_sem, recv_sem, local_sem)
        )


def exchange_body(axis, n, gather, x_ref, o_ref, send_sem, recv_sem, local_sem):
    me = lax.axis_index(axis)
    barrier = pltpu.get_barrier_semaphore()
    for j in range(1, n):
        pl.semaphore_signal(
            barrier, 1, device_id={axis: (me + j) % n}, device_id_type=pl.DeviceIdType.MESH
        )
    pl.semaphore_wait(barrier, n - 1)
    copies = []
    for j in range(1, n):
        peer = (me + j) % n
        copy = pltpu.make_async_remote_copy(
            src_ref=x_ref if gather else x_ref.at[peer],
            dst_ref=o_ref.at[me],
            send_sem=send_sem.at[j],
            recv_sem=recv_sem.at[j],
            device_id={axis: peer},
            device_id_type=pl.DeviceIdType.MESH,
        )
        copy.start()
        copies.append(copy)
    local = pltpu.make_async_copy(x_ref if gather else x_ref.at[me], o_ref.at[me], local_sem)
    local.start()
    local.wait()
    for copy in copies:
        copy.wait()


def exchange(x, axis, collective_id, gather=False, gate=None):
    n = lax.axis_size(axis)
    out_shape = (n,) + x.shape if gather else x.shape
    return pl.pallas_call(
        functools.partial(exchange_kernel, axis, n, gather, gate),
        out_shape=jax.ShapeDtypeStruct(out_shape, x.dtype),
        in_specs=[pl.BlockSpec(memory_space=pl.ANY)],
        out_specs=pl.BlockSpec(memory_space=pl.ANY),
        scratch_shapes=[
            pltpu.SemaphoreType.DMA((n,)),
            pltpu.SemaphoreType.DMA((n,)),
            pltpu.SemaphoreType.DMA(()),
        ],
        compiler_params=pltpu.CompilerParams(collective_id=collective_id, has_side_effects=True),
    )(x)


def rotate(key_vecs, positions):
    half_dim = key_vecs.shape[-1] // 2
    inv_freq = jnp.exp(
        -math.log(500000.0) * (2.0 * jnp.arange(half_dim, dtype=jnp.float32) / key_vecs.shape[-1])
    )
    angles = positions.astype(jnp.float32)[..., None, None] * inv_freq
    cos_vals = jnp.cos(angles)
    sin_vals = jnp.sin(angles)
    front_half = key_vecs[..., :half_dim]
    back_half = key_vecs[..., half_dim:]
    return jnp.concatenate(
        [
            front_half * cos_vals - back_half * sin_vals,
            back_half * cos_vals + front_half * sin_vals,
        ],
        axis=-1,
    )


def body(
    hidden,
    queries,
    norm_gain,
    kv_weight,
    adapter_in,
    adapter_out,
    kv_pages,
    adapter_ids,
    owner_rows,
    page_table,
    lengths,
    moves,
):
    section_count = lax.axis_size("pipe")
    req_count = lax.axis_size("req")
    section_id = lax.axis_index("pipe")
    my_req = lax.axis_index("req")
    width_loc = hidden.shape[1]
    q_width = queries.shape[2]
    kv_width = kv_weight.shape[3]
    kv_heads = kv_width // HD
    group_size = q_width // HD // kv_heads
    batches = 1
    per_batch = RQ // batches
    rows_per = per_batch * S
    block_cap = min(RQ_MB, max(2, 2 * RQ_MB // req_count))
    batch_cap = block_cap * (MICRO // batches)
    pair_cap = (MOVES + req_count - 2) // (req_count - 1)
    free_slots = (req_count - 1) * pair_cap
    token_ids = jnp.arange(S, dtype=jnp.int32)
    store_rows = owner_rows[adapter_ids]
    dest_all = store_rows // ADP_DEV
    pick_all = store_rows % ADP_DEV
    req_ids = jnp.arange(RQ, dtype=jnp.int32)
    earlier = (
        (req_ids[None, :] < req_ids[:, None])
        & (req_ids[None, :] // per_batch == req_ids[:, None] // per_batch)
        & (dest_all[None, :] == dest_all[:, None])
    )
    slot_all = jnp.sum(earlier.astype(jnp.int32), axis=1)
    positions = (lengths[:, None] + token_ids[None, :]).reshape(RQ * S)
    gain_full = norm_gain[0].astype(jnp.float32)
    weight_flat = kv_weight[0].reshape(D, 2 * kv_width)
    layer_pages = kv_pages[0]
    adapters_in = adapter_in[0]
    adapters_out = adapter_out[0].reshape(ADP_DEV * R, width_loc)
    key_pos = jnp.arange(CTX, dtype=jnp.int32)
    causal = token_ids[None, :] <= token_ids[:, None]
    adapter_slots = jnp.arange(ADP_DEV, dtype=jnp.int32)
    move_ids = jnp.arange(MOVES, dtype=jnp.int32)
    move_dest = moves[:, 0]
    move_slot = jnp.sum(
        (
            (move_ids[None, :] < move_ids[:, None]) & (move_dest[None, :] == move_dest[:, None])
        ).astype(jnp.int32),
        axis=1,
    )
    picks_out = jnp.zeros((req_count, batch_cap), jnp.int32).at[dest_all, slot_all].set(pick_all)
    spots_out = jnp.full((req_count, pair_cap), -1, jnp.int32).at[move_dest, move_slot].set(moves[:, 2])
    ints_in = lax.all_to_all(
        jnp.concatenate([picks_out, spots_out], axis=1), "req", split_axis=0, concat_axis=0, tiled=True
    )
    picks_in = ints_in[:, :batch_cap]
    spots_in = ints_in[:, batch_cap:].reshape(req_count * pair_cap)
    spot_match = spots_in[None, :] == jnp.arange(free_slots, dtype=jnp.int32)[:, None]
    has_page = jnp.any(spot_match, axis=1)
    page_src = jnp.argmax(spot_match, axis=1)
    box_ids = jnp.arange(req_count * pair_cap, dtype=jnp.int32)
    box_match = (move_dest * pair_cap + move_slot)[None, :] == box_ids[:, None]
    box_move = jnp.argmax(box_match, axis=1)
    box_used = jnp.any(box_match, axis=1)
    box_page = jnp.where(box_used, moves[box_move, 1], -1)
    box_pick = (box_page[:, None] == jnp.arange(layer_pages.shape[0], dtype=jnp.int32)[None, :]).astype(
        jnp.bfloat16
    )
    land_pick = (spot_match & has_page[:, None]).astype(jnp.bfloat16)
    box_count = req_count * pair_cap

    def build_pages(fresh):
        spot_ids = jnp.arange(req_count * pair_cap * PAGE, dtype=jnp.int32)
        tok_match = tok_spot[None, :] == spot_ids[:, None]
        tok_pick = tok_match.astype(jnp.bfloat16)
        tok_hit = jnp.any(tok_match, axis=1).reshape(req_count * pair_cap, PAGE)
        base = jnp.einsum(
            "bp,pcjk->bcjk", box_pick, layer_pages, preferred_element_type=jnp.float32
        ).astype(jnp.bfloat16)
        patch = jnp.einsum(
            "bjt,tck->bcjk",
            tok_pick.reshape(box_count, PAGE, RQ * S),
            fresh,
            preferred_element_type=jnp.float32,
        ).astype(jnp.bfloat16)
        return jnp.where(tok_hit[:, None, :, None], patch, base).reshape(
            req_count, pair_cap, 2, PAGE, kv_width
        )

    def no_pages(fresh):
        return jnp.zeros((req_count, pair_cap, 2, PAGE, kv_width), jnp.bfloat16)

    arrived = jnp.zeros((free_slots, 2, PAGE, kv_width), jnp.bfloat16)
    page_slot = jnp.take_along_axis(page_table, (positions // PAGE).reshape(RQ, S), axis=1).reshape(
        RQ * S
    )
    tok_in_box = page_slot[:, None] == box_page[None, :]
    tok_spot = jnp.where(
        jnp.any(tok_in_box, axis=1),
        jnp.argmax(tok_in_box, axis=1).astype(jnp.int32) * PAGE + positions % PAGE,
        -1,
    )
    tp_count = lax.axis_size("tp")
    my_tp = lax.axis_index("tp")
    gain_own = lax.dynamic_slice_in_dim(gain_full, my_tp * width_loc, width_loc)
    weight_own = kv_weight[0].reshape(D, 2 * kv_width)

    def shuffle_rows(weight_src):
        relative_rows = [lax.dynamic_slice_in_dim(weight_src, my_tp * width_loc, width_loc, axis=0)]
        later = [(p * tp_count + t) for p in range(1, section_count) for t in range(tp_count)]
        for shift in range(1, tp_count):
            outgoing_rows = lax.dynamic_slice_in_dim(
                weight_src, ((my_tp + shift) % tp_count) * width_loc, width_loc, axis=0
            )
            route = [(i, i - i % tp_count + (i % tp_count + shift) % tp_count) for i in later]
            relative_rows.append(lax.ppermute(outgoing_rows, ("pipe", "tp"), route))
        return jnp.concatenate(relative_rows, axis=1)
    block_order = (my_tp - jnp.arange(tp_count, dtype=jnp.int32)) % tp_count
    carried = jnp.zeros((rows_per, width_loc), jnp.bfloat16)
    section_rows = jnp.zeros((RQ * S, width_loc), jnp.bfloat16)
    fresh_rows = jnp.zeros((RQ * S, 2, kv_width), jnp.bfloat16)
    for tick_id in range(batches + section_count - 1):
        offset_batch = tick_id - section_id
        active = (offset_batch >= 0) & (offset_batch < batches)
        if tick_id == 0:
            hstate = hidden
            whole_rows = lax.all_gather(hstate, "tp", axis=1, tiled=True)
            widened = whole_rows.astype(jnp.float32)
            inv_rms = lax.rsqrt(jnp.mean(widened * widened, axis=-1, keepdims=True) + 1e-05)
            normed = (widened * inv_rms * gain_full).astype(jnp.bfloat16)
            projected = jnp.dot(normed, weight_flat, preferred_element_type=jnp.float32)
        else:
            hstate = carried
            widened = hstate.astype(jnp.float32)
            scaled = (widened * gain_own).astype(jnp.bfloat16)
            part_rel = jnp.dot(scaled, weight_rows, preferred_element_type=jnp.float32).reshape(
                rows_per, tp_count, 2 * kv_width
            )
            part_abs = jnp.swapaxes(jnp.take(part_rel, block_order, axis=1), 0, 1)
            sumsq = jnp.sum(widened * widened, axis=-1)
            sumsq_rows = jnp.zeros((tp_count, 8, 2 * kv_width), jnp.float32).at[:, 0, :rows_per].set(
                jnp.broadcast_to(sumsq, (tp_count, rows_per))
            )
            got = exchange(
                jnp.concatenate([part_abs, sumsq_rows], axis=1), "tp", 10 + tick_id, gate=tick_id
            )
            got = jnp.sum(got, axis=0)
            inv_rms = lax.rsqrt(got[rows_per, :rows_per] / D + 1e-05)
            projected = got[:rows_per] * inv_rms[:, None]
        projected = projected.reshape(rows_per, 2, kv_heads, HD)
        new_keys = rotate(projected[:, 0], positions).astype(jnp.bfloat16)
        new_values = projected[:, 1].astype(jnp.bfloat16)
        fresh_kv = jnp.stack(
            [new_keys.reshape(rows_per, kv_width), new_values.reshape(rows_per, kv_width)], axis=1
        )
        gathered = layer_pages[page_table]
        cached = jnp.swapaxes(gathered, 1, 2).reshape(per_batch, 2, CTX, kv_heads, HD)
        fresh_heads = fresh_kv.reshape(per_batch, S, 2, kv_heads, HD)
        query_heads = queries[0].reshape(per_batch, S, kv_heads, group_size, HD)
        score_old = jnp.einsum(
            "bskgd,btkd->bskgt", query_heads, cached[:, 0], preferred_element_type=jnp.float32
        ) * HD ** (-0.5)
        score_new = jnp.einsum(
            "bskgd,btkd->bskgt",
            query_heads,
            fresh_heads[:, :, 0],
            preferred_element_type=jnp.float32,
        ) * HD ** (-0.5)
        old_ok = key_pos[None, :] < lengths[:, None]
        score_old = jnp.where(old_ok[:, None, None, None, :], score_old, -jnp.inf)
        score_new = jnp.where(causal[None, :, None, None, :], score_new, -jnp.inf)
        row_max = jnp.maximum(jnp.max(score_old, axis=-1), jnp.max(score_new, axis=-1))[..., None]
        exp_old = jnp.exp(score_old - row_max)
        exp_new = jnp.exp(score_new - row_max)
        denominator = (jnp.sum(exp_old, axis=-1) + jnp.sum(exp_new, axis=-1))[..., None]
        weight_old = (exp_old / denominator).astype(jnp.bfloat16)
        weight_new = (exp_new / denominator).astype(jnp.bfloat16)
        mixed = jnp.einsum(
            "bskgt,btkd->bskgd", weight_old, cached[:, 1], preferred_element_type=jnp.float32
        )
        mixed = mixed + jnp.einsum(
            "bskgt,btkd->bskgd",
            weight_new,
            fresh_heads[:, :, 1],
            preferred_element_type=jnp.float32,
        )
        attended = mixed.reshape(per_batch, S, q_width).astype(jnp.bfloat16)
        outgoing = (
            jnp.zeros((req_count, batch_cap, S, q_width), jnp.bfloat16)
            .at[dest_all, slot_all]
            .set(attended)
        )
        rows_in = exchange(outgoing, "req", 20 + tick_id, gate=tick_id)
        sources = rows_in.shape[0]
        item_count = rows_in.shape[1]
        flat_rows = rows_in.reshape(sources * item_count * S, q_width)
        all_low = jnp.einsum(
            "nf,arf->nar", flat_rows, adapters_in, preferred_element_type=jnp.float32
        )
        picks_rows = jnp.broadcast_to(picks_in[:, :, None], (sources, item_count, S)).reshape(
            sources * item_count * S
        )
        one_hot = (picks_rows[:, None] == adapter_slots[None, :]).astype(jnp.float32)
        partial_low = jnp.sum(all_low * one_hot[:, :, None], axis=1)
        rank_low = jnp.sum(exchange(partial_low, "tp", 30 + tick_id, gather=True, gate=tick_id), axis=0).astype(jnp.bfloat16)
        spread = (rank_low.astype(jnp.float32)[:, None, :] * one_hot[:, :, None]).astype(
            jnp.bfloat16
        )
        deltas = jnp.dot(
            spread.reshape(sources * item_count * S, ADP_DEV * R),
            adapters_out,
            preferred_element_type=jnp.float32,
        ).astype(jnp.bfloat16)
        deltas = deltas.reshape(sources, item_count, S, width_loc)
        returned = exchange(deltas, "req", 40 + tick_id, gate=tick_id)
        delta_rows = returned[dest_all, slot_all].reshape(rows_per, width_loc)
        new_state = (hstate.astype(jnp.float32) + delta_rows.astype(jnp.float32)).astype(
            jnp.bfloat16
        )
        section_rows = jnp.where(active, new_state, section_rows)
        fresh_rows = jnp.where(active, fresh_kv, fresh_rows)
        if tick_id + 1 < section_count:
            carried = passed_along(new_state, "pipe", tick_id)
        if tick_id == 0:
            weight_src, _ = lax.optimization_barrier((weight_own, new_state))
            weight_rows = shuffle_rows(weight_src)
        sent_pages = lax.cond(section_id == tick_id, build_pages, no_pages, fresh_kv)
        got_pages = exchange(sent_pages, "req", 50 + tick_id, gate=tick_id)
        landed = jnp.einsum(
            "fb,bcjk->fcjk",
            land_pick,
            got_pages.reshape(box_count, 2, PAGE, kv_width),
            preferred_element_type=jnp.float32,
        ).astype(jnp.bfloat16)
        arrived = jnp.where(section_id == tick_id, landed, arrived)

    return (section_rows[None], fresh_rows[None], arrived[None])


def solution(mesh):
    in_specs = (
        P("req", "tp"),
        P("pipe", "req", "tp"),
        P("pipe", None),
        P("pipe", None, None, "tp"),
        P("pipe", "req", None, "tp"),
        P("pipe", "req", None, "tp"),
        P("pipe", "req", None, None, "tp"),
        P("req"),
        P(),
        P("req", None),
        P("req"),
        P("req", None),
    )
    out_specs = (
        P("pipe", "req", "tp"),
        P("pipe", "req", None, "tp"),
        P("pipe", "req", None, None, "tp"),
    )
    return jax.shard_map(body, mesh=mesh, in_specs=in_specs, out_specs=out_specs, check_vma=False)
```
